256 devices in a mesh: dp: 64 (over z, x, core), section: 4 (over y).
Axes of the slice: x: 4, y: 4, z: 8, core: 2. Of those that a mesh axis runs over, the one named last changes fastest.
Arguments:
- token_ids: int32 [4, 64, 128], P('section', 'dp'), may hold values from 0 to 511
- segment_ids: int32 [4, 64, 128], P('section', 'dp'), may hold values from 0 to 3, never falling along the last dimension, each value on 1 to 64 neighbouring positions
- row_order: int32 [4, 64], P('section', 'dp'), may hold values from 0 to 63, each once within a row
- embed_table: bfloat16 [4, 512, 4096], P('section'), may hold values from -6 to 6
- norm_gain: float32 [4, 4096], P('section'), may hold values from 0.5 to 2
- position_bias: float32 [4, 32, 64], P('section'), may hold values from -4 to 4
- returned_grad: bfloat16 [4, 8192, 4096], P('section', 'dp'), may hold values from -6 to 6
Outputs:
- handed: bfloat16 [4, 8192, 4096], P('section', 'dp')
- grad_table: float32 [4, 512, 4096], P('section', 'dp')
- grad_gain: float32 [4, 4096], P('section')
- grad_bias: float32 [4, 32, 64], P('section')
The draws below stay inside these ranges and needn't reach their ends.
All inputs are finite; a program needn't handle non-finite values.
Results may differ from the reference program's by a relative error of at most 0.014.
Values may be sent and summed in bfloat16 or wider, within the bound.
No kernel may reach another device: no remote copies, remote signals or barrier semaphores. Data moves between devices by JAX's collectives and lax.ppermute only.
A program may use at most 128 MiB of HBM per device.

```python
import math
import jax
import jax.numpy as jnp
import numpy as np
from jax import lax

D = 4096
HEADS = 64
VOCAB = 512
ROW_LEN = 128
BUCKETS = 32
ROWS = 64
TOKENS = 8192
N_SECTION = 4


def set_ends(entries, key, low, top_value):
    index_at = [jax.random.randint(jax.random.fold_in(key, axis), (), 0, length) for axis, length in enumerate(entries.shape)]
    widest = entries.shape.index(max(entries.shape))
    next_to = index_at[:widest] + [(index_at[widest] + 1) % entries.shape[widest]] + index_at[widest + 1:]
    return entries.at[tuple(index_at)].set(low).at[tuple(next_to)].set(top_value)


def steps_of(stream_key, dims, shards, least, largest):
    def one(dim, parts):
        heights = jax.random.uniform(jax.random.fold_in(jax.random.fold_in(stream_key, 6), dim), (parts,), jnp.float32, least / len(shards), largest / len(shards))
        return jnp.repeat(jnp.exp(heights), dims[dim] // parts).reshape((-1,) + (1,) * (len(dims) - dim - 1))

    level = one(*shards[0])
    for cut in shards[1:]:
        level = level * one(*cut)
    return level


def profile(number_of, total, bound, lean):
    loads = [(1 << 20) // math.isqrt(grade ** lean) + 1 for grade in range(2, number_of + 1)]
    surplus, given = total - bound - (number_of - 1), [1] * (number_of - 1)
    while surplus > 0:
        free = [i for i in range(number_of - 1) if given[i] < bound]
        pool, left = sum([loads[i] for i in free]), surplus
        for i in free:
            extra = min(bound - given[i], max(1, left * loads[i] // pool), surplus)
            given[i] = given[i] + extra
            surplus = surplus - extra
    return np.array([bound] + given)


def uneven_parts(rng, number_of, total, reach, slope):
    if number_of == 2:
        one = jax.random.randint(rng, (), max(1, total - reach), min(reach, total - 1) + 1)
        return jnp.stack([one, total - one])
    lengths = jnp.asarray(profile(number_of, total, reach, slope), jnp.int32)
    couples = (number_of - 1) // 2
    donor, receiver = lengths[1:1 + 2 * couples:2], lengths[2:2 + 2 * couples:2]
    margin = jnp.minimum(donor - 1, reach - receiver)
    shifted = jax.random.randint(jax.random.fold_in(rng, 1), (couples,), 0, 1 << 20) % (margin + 1)
    lengths = lengths.at[1:1 + 2 * couples:2].set(donor - shifted).at[2:2 + 2 * couples:2].set(receiver + shifted)
    return lengths[jax.random.permutation(jax.random.fold_in(rng, 2), number_of)]


def noise(own_key, dims, scale, bound, cuts=(), kind=jnp.bfloat16):
    drawn = scale * jax.random.normal(own_key, dims, jnp.float32)
    if cuts:
        drawn = drawn * steps_of(own_key, dims, cuts, -0.22, 0.18)
    return jnp.clip(drawn, -bound, bound).astype(kind)


def setup_inputs(seed: int = 0) -> dict:
    seeds = jax.random.split(jax.random.key(seed), 8)
    token_ids = set_ends(jax.random.randint(seeds[0], (N_SECTION, ROWS, ROW_LEN), 0, VOCAB), jax.random.fold_in(seeds[0], 1), 0, VOCAB - 1).astype(jnp.int32)
    segment_ids = jax.vmap(lambda own: jnp.searchsorted(jnp.cumsum(uneven_parts(own, 4, ROW_LEN, 64, 2)), jnp.arange(ROW_LEN), side="right"))(jax.random.split(seeds[1], N_SECTION * ROWS)).reshape((N_SECTION, ROWS, ROW_LEN)).astype(jnp.int32)
    row_order = jax.vmap(lambda own: jax.random.permutation(own, ROWS))(jax.random.split(seeds[2], N_SECTION)).reshape((N_SECTION, ROWS)).astype(jnp.int32)
    embed_table = noise(seeds[3], (N_SECTION, VOCAB, D), 1.0, 6.0, ((0, 4),))
    norm_gain = jnp.clip(jnp.exp(math.log(2.0) - 1.3862944 * jax.random.uniform(seeds[4], (N_SECTION, D), jnp.float32) ** steps_of(seeds[4], (N_SECTION, D), ((0, 4),), -0.2, 0.2)), 0.5, 2.0)
    position_bias = noise(seeds[5], (N_SECTION, BUCKETS, HEADS), 1.0, 4.0, ((0, 4),), jnp.float32)
    returned_grad = noise(seeds[6], (N_SECTION, TOKENS, D), 1.0, 6.0, ((0, 4), (1, 64)))
    return dict(token_ids=token_ids, segment_ids=segment_ids, row_order=row_order, embed_table=embed_table, norm_gain=norm_gain, position_bias=position_bias, returned_grad=returned_grad)


limits = (12, 16, 23, 32, 45, 64, 91)

def bucket_table(length):
    places = jnp.arange(length, dtype=jnp.int32)
    offset = places[None, :] - places[:, None]
    apart = jnp.abs(offset)
    bucket = jnp.minimum(apart, 8)
    for limit in limits:
        bucket = bucket + (apart >= limit).astype(jnp.int32)
    bucket = bucket + 16 * (offset > 0).astype(jnp.int32)
    return bucket

def attend_row(row_normed, row_segs, bias_full, heads, head_size):
    length = row_normed.shape[0]
    split = row_normed.reshape(length, heads, head_size).astype(jnp.float32)
    scores = jnp.einsum('qhd,khd->hqk', split, split) / head_size + bias_full
    same = row_segs[:, None] == row_segs[None, :]
    scores = jnp.where(same[None, :, :], scores, -1e+30)
    top = lax.optimization_barrier(jnp.max(scores, axis=-1, keepdims=True))
    expo = jnp.exp(scores - top)
    probs = (expo / lax.optimization_barrier(jnp.sum(expo, axis=-1, keepdims=True))).astype(jnp.bfloat16)
    mixed = jnp.einsum('hqk,khd->qhd', probs.astype(jnp.float32), split)
    return mixed.reshape(length, heads * head_size)

def layer(embedded, gain, bias, segs):
    rows_count, length = segs.shape
    width = embedded.shape[1]
    heads = bias.shape[1]
    head_size = width // heads
    wide = embedded.astype(jnp.float32)
    meansq = lax.optimization_barrier(jnp.mean(wide * wide, axis=-1, keepdims=True))
    normed = (wide * lax.rsqrt(meansq + 1e-06) * gain).astype(jnp.bfloat16)
    picks = (bucket_table(length)[:, :, None] == jnp.arange(bias.shape[0], dtype=jnp.int32)).astype(jnp.float32)
    bias_full = jnp.einsum('qkb,bh->hqk', picks, bias)
    blocks = normed.reshape(rows_count, length, width)
    mixed = lax.map(lambda pair: attend_row(pair[0], pair[1], bias_full, heads, head_size), (blocks, segs))
    return (wide + mixed.reshape(rows_count * length, width)).astype(jnp.bfloat16)

def reference(token_ids, segment_ids, row_order, embed_table, norm_gain, position_bias, returned_grad):
    sections = token_ids.shape[0]
    outputs = []
    tables = []
    gains = []
    biases = []
    for section in range(sections):
        order = row_order[section]
        packed = token_ids[section][order]
        segs = segment_ids[section][order]
        onehot = (packed.reshape(-1)[:, None] == jnp.arange(VOCAB, dtype=jnp.int32)[None, :]).astype(jnp.bfloat16)
        embedded = jnp.dot(onehot, embed_table[section], preferred_element_type=jnp.float32).astype(jnp.bfloat16)
        result, pullback = jax.vjp(lambda first, second, third: layer(first, second, third, segs), embedded, norm_gain[section], position_bias[section])
        grad_rows, grad_g, grad_b = pullback(returned_grad[(section + 1) % sections])
        table_term = jnp.dot(onehot.T, grad_rows, preferred_element_type=jnp.float32)
        outputs.append(result)
        tables.append(table_term)
        gains.append(grad_g)
        biases.append(grad_b)
    handed = jnp.stack([outputs[(section - 1) % sections] for section in range(sections)])
    return (handed, jnp.stack(tables), jnp.stack(gains), jnp.stack(biases))
```

```python
import functools

import jax
import jax.numpy as jnp
import numpy as np
from jax import lax
from jax.experimental import pallas as pl
from jax.experimental.pallas import tpu as pltpu
from jax.sharding import Mesh, PartitionSpec as P

F32, BF16 = jnp.float32, jnp.bfloat16
LIMITS = (12, 16, 23, 32, 45, 64, 91)
LOG2E = 1.4426950408889634
L = 128
NX = 4
BIG = 56 * 1024 * 1024


def bucket_picks():
    c = np.arange(L)
    r = np.where(c < 64, c, c - L)
    a = np.abs(r)
    b = np.minimum(a, 8) + sum((a >= t).astype(np.int64) for t in LIMITS) + 16 * (r > 0)
    return (np.arange(32)[:, None] == b[None, :]).astype(np.float32)


def dot(a, b, dims, precision=None):
    return lax.dot_general(a, b, (dims, ((), ())), precision=precision, preferred_element_type=F32)


NN, NT, TN = ((1,), (0,)), ((1,), (1,)), ((0,), (0,))


def halves(tile):
    low = lax.broadcasted_iota(jnp.int32, tile.shape, 1) < 64
    zero = jnp.zeros_like(tile)
    return jnp.concatenate([jnp.where(low, tile, zero), jnp.where(low, zero, tile)], axis=0)


def offset_sums(square):
    acc = square[:8]
    for k in range(8, L, 8):
        acc = acc + pltpu.roll(square[k : k + 8], L - k, 1)
    row = lax.broadcasted_iota(jnp.int32, acc.shape, 0)
    for bit in (1, 2, 4):
        acc = jnp.where((row & bit) != 0, pltpu.roll(acc, L - bit, 1), acc)
    return jnp.sum(acc, axis=0, keepdims=True)


def pre_kernel(x_ref, table_ref, gain_ref, pos_ref, picks_ref, ne_ref, r_ref, bvec_ref):
    width = table_ref.shape[1]
    part = width // NX
    wide = table_ref[...].astype(F32)
    r = lax.rsqrt(jnp.sum(wide * wide, axis=1, keepdims=True) * (1.0 / width) + 1e-06)
    r_ref[...] = jnp.broadcast_to(r, r_ref.shape)
    cols = pl.ds(pl.multiple_of(x_ref[0] * part, L), part)
    own = table_ref[:, cols]
    ne_ref[:, :part] = (own.astype(F32) * r * gain_ref[:, cols]).astype(BF16)
    ne_ref[:, part:] = own
    bvec_ref[...] = dot(pos_ref[...], picks_ref[...], TN, lax.Precision.HIGHEST) * LOG2E


def prepare(x, table, gain, pos, picks):
    vocab, width = table.shape
    part = width // NX
    rows = 64
    heads = pos.shape[1]
    return pl.pallas_call(
        pre_kernel,
        grid_spec=pltpu.PrefetchScalarGridSpec(
            num_scalar_prefetch=1,
            grid=(vocab // rows,),
            in_specs=[
                pl.BlockSpec((rows, width), lambda i, x: (i, 0)),
                pl.BlockSpec((1, width), lambda i, x: (0, 0)),
                pl.BlockSpec(pos.shape, lambda i, x: (0, 0)),
                pl.BlockSpec(picks.shape, lambda i, x: (0, 0)),
            ],
            out_specs=[
                pl.BlockSpec((rows, 2 * part), lambda i, x: (i, 0)),
                pl.BlockSpec((rows, L), lambda i, x: (i, 0)),
                pl.BlockSpec((heads, L), lambda i, x: (0, 0)),
            ],
        ),
        out_shape=[
            jax.ShapeDtypeStruct((vocab, 2 * part), BF16),
            jax.ShapeDtypeStruct((vocab, L), F32),
            jax.ShapeDtypeStruct((heads, L), F32),
        ],
        cost_estimate=pl.CostEstimate(flops=vocab * width * 4, bytes_accessed=7 << 20, transcendentals=0),
        name="prepare",
    )(x, table, gain, pos, picks)


def onehot_t(ids_row, vocab):
    v = lax.broadcasted_iota(jnp.int32, (vocab, ids_row.shape[1]), 0)
    return jnp.where(v == ids_row, 1.0, 0.0).astype(BF16)


def fwd_kernel(where_ref, order_ref, ids_ref, segs_ref, ne_ref, bvec_ref, *rest):
    a_refs, (n_ref, p_ref), (e_ref, m_ref) = rest[:NX], rest[NX : NX + 2], rest[NX + 2 :]
    part = ne_ref.shape[1] // 2
    vocab = ne_ref.shape[0]
    pairs = part // L
    for s in range(NX):
        row = order_ref[where_ref[1 + s]]
        both = dot(onehot_t(ids_ref[pl.ds(row, 1), :], vocab), ne_ref[...], TN)
        n_ref[s] = both[:, :part].astype(BF16)
        e_ref[s] = both[:, part:].astype(BF16)
        seg = jnp.broadcast_to(segs_ref[pl.ds(row, 1), :], (L, L)).astype(F32)
        m_ref[s] = jnp.where(seg == seg.T, 0.0, -1e30)

    @pl.loop(0, pairs)
    def _(p):
        cols = pl.ds(pl.multiple_of(p * L, L), L)
        head = where_ref[0] * (2 * pairs) + 2 * p
        biases = [
            pltpu.roll(
                jnp.broadcast_to(bvec_ref[pl.ds(head + k, 1), :], (L, L)), 0, 1, stride=1, stride_axis=0
            )
            for k in range(2)
        ]
        for s in range(NX):
            tile = n_ref[s, :, cols]
            two = halves(tile)
            mask = m_ref[s]
            scores = dot(two, tile, NT) * (LOG2E / 64.0)
            scores = scores + jnp.concatenate([biases[0] + mask, biases[1] + mask], axis=0)
            expo = jnp.exp2(scores - jnp.max(scores, axis=1, keepdims=True))
            probs = (expo * (1.0 / jnp.sum(expo, axis=1, keepdims=True))).astype(BF16)
            p_ref[p, s] = probs
            mixed = dot(jnp.concatenate([probs[:L], probs[L:]], axis=1), two, NN)
            a_refs[s][:, cols] = (e_ref[s, :, cols].astype(F32) + mixed).astype(BF16)


def forward(where, order, ids, segs, ne, bvec):
    part = ne.shape[1] // 2
    pairs = part // L
    smem, vmem = pl.BlockSpec(memory_space=pltpu.SMEM), pl.BlockSpec(memory_space=pltpu.VMEM)
    return pl.pallas_call(
        fwd_kernel,
        in_specs=[smem, smem, vmem, vmem, vmem, vmem],
        out_specs=[vmem] * (NX + 2),
        out_shape=[jax.ShapeDtypeStruct((L, part), BF16)] * NX
        + [
            jax.ShapeDtypeStruct((NX, L, part), BF16),
            jax.ShapeDtypeStruct((pairs, NX, 2 * L, L), BF16),
        ],
        scratch_shapes=[pltpu.VMEM((NX, L, part), BF16), pltpu.VMEM((NX, L, L), F32)],
        compiler_params=pltpu.CompilerParams(vmem_limit_bytes=BIG),
        cost_estimate=pl.CostEstimate(flops=2 << 30, bytes_accessed=8 << 20, transcendentals=1 << 20),
        name="forward",
    )(where, order, ids, segs, ne, bvec)


def bwd_kernel(where_ref, order_ref, ids_ref, ne_ref, r_ref, gain_ref, picks_ref, n_ref, p_ref, *rest):
    g_refs, (mine_ref, other_ref), (d_ref, rg_ref, o_ref, diag_ref) = rest[:NX], rest[NX : NX + 2], rest[NX + 2 :]
    vocab, part = ne_ref.shape[0], ne_ref.shape[1] // 2
    pairs = part // L
    blocks = vocab // 16
    core = where_ref[5]

    @pl.loop(0, pairs)
    def _(p):
        cols = pl.ds(pl.multiple_of(p * L, L), L)
        total = jnp.zeros((2 * L, L), F32)
        for s in range(NX):
            tile, up = n_ref[s, :, cols], g_refs[s][:, cols]
            rg_ref[pl.ds(s * L, L), cols] = up
            two, ups = halves(tile), halves(up)
            probs = p_ref[p, s]
            wide = probs.astype(F32)
            d_probs = dot(ups, tile, NT).astype(BF16).astype(F32)
            both = wide * d_probs
            d_scores = both - wide * jnp.sum(both, axis=1, keepdims=True)
            total = total + d_scores
            small = (d_scores * (1.0 / 64.0)).astype(BF16)
            left = jnp.concatenate([probs, small], axis=0)
            right = jnp.concatenate([ups, two], axis=0)
            d_norm = dot(left, right, TN)
            d_norm = d_norm + dot(jnp.concatenate([small[:L], small[L:]], axis=1), two, NN)
            d_ref[pl.ds(s * L, L), cols] = d_norm.astype(BF16)
        for k in range(2):
            diag_ref[pl.ds(2 * p + k, 1), :] = offset_sums(total[k * L : (k + 1) * L])

    for s in range(NX):
        row = order_ref[where_ref[1 + s]]
        o_ref[:, s * L : (s + 1) * L] = onehot_t(ids_ref[pl.ds(row, 1), :], vocab)

    def put(tile, value):
        value = value.reshape(blocks, 2, 8, L)
        first, second = value[:, 0], value[:, 1]
        mine_ref[0:blocks, tile] = jnp.where(core == 0, first, second)
        other_ref[0:blocks, tile] = jnp.where(core == 0, second, first)

    r = r_ref[...]
    along = jnp.zeros((vocab, L), F32)
    for f in range(pairs):
        cols = slice(f * L, (f + 1) * L)
        d_act = dot(o_ref[...], rg_ref[:, cols], NN)
        d_norm = dot(o_ref[...], d_ref[:, cols], NN)
        gain = gain_ref[:, cols]
        own = ne_ref[:, part + f * L : part + (f + 1) * L].astype(F32)
        scaled = d_norm * r
        put(f, d_act + scaled * gain)
        along = along + own * (d_norm * gain)
        g_row = jnp.sum(own * scaled, axis=0, keepdims=True)
        mine_ref[blocks, 0, pl.ds(f, 1), :] = g_row
        other_ref[blocks, 0, pl.ds(f, 1), :] = g_row
    put(pairs, along)
    sums = dot(diag_ref[...], picks_ref[...], NT, lax.Precision.HIGHEST)
    for ref in (mine_ref, other_ref):
        ref[blocks, 1] = sums[:8]
        ref[blocks, 2] = sums[8:]
        for tile in range(3, pairs + 1):
            ref[blocks, tile] = jnp.zeros((8, L), F32)


def backward(where, order, ids, ne, r, gain, picks, n, probs, grads):
    vocab, part = ne.shape[0], ne.shape[1] // 2
    pairs = part // L
    smem, vmem = pl.BlockSpec(memory_space=pltpu.SMEM), pl.BlockSpec(memory_space=pltpu.VMEM)
    out = jax.ShapeDtypeStruct((vocab // 16 + 1, pairs + 1, 8, L), F32)
    return pl.pallas_call(
        bwd_kernel,
        in_specs=[smem, smem] + [vmem] * (7 + NX),
        out_specs=[vmem, vmem],
        out_shape=[out, out],
        scratch_shapes=[
            pltpu.VMEM((NX * L, part), BF16),
            pltpu.VMEM((NX * L, part), BF16),
            pltpu.VMEM((vocab, NX * L), BF16),
            pltpu.VMEM((2 * pairs, L), F32),
        ],
        compiler_params=pltpu.CompilerParams(vmem_limit_bytes=BIG),
        cost_estimate=pl.CostEstimate(flops=4 << 30, bytes_accessed=10 << 20, transcendentals=0),
        name="backward",
    )(where, order, ids, ne, r, gain, picks, n, probs, *grads)


def join_kernel(mine_ref, came_ref, out_ref):
    blocks, tiles = mine_ref.shape[0] - 1, mine_ref.shape[1]
    for t in range(tiles):
        out_ref[:, t] = (mine_ref[0:blocks, t] + came_ref[0:blocks, t]).astype(BF16)
    for t in range(3):
        value = mine_ref[blocks, t] + came_ref[blocks, t]
        high = value.astype(BF16)
        out_ref[:, tiles + t] = jnp.broadcast_to(high[None], (blocks, 8, L))
        low = (value - high.astype(F32)).astype(BF16)
        out_ref[:, tiles + 3 + t] = jnp.broadcast_to(low[None], (blocks, 8, L))


def join(mine, came):
    blocks, tiles = mine.shape[0] - 1, mine.shape[1]
    vmem = pl.BlockSpec(memory_space=pltpu.VMEM)
    return pl.pallas_call(
        join_kernel,
        in_specs=[vmem, vmem],
        out_specs=vmem,
        out_shape=jax.ShapeDtypeStruct((blocks, tiles + 6, 8, L), BF16),
        compiler_params=pltpu.CompilerParams(vmem_limit_bytes=BIG),
        cost_estimate=pl.CostEstimate(flops=1 << 20, bytes_accessed=4 << 20, transcendentals=0),
        name="join",
    )(mine, came)


def last_kernel(where_ref, parts_ref, table_ref, r_ref, t_ref, g_ref, b_ref, h_ref):
    sources, tiles = parts_ref.shape[0], parts_ref.shape[1]
    feats = tiles - 7
    width = table_ref.shape[1]

    def total(x, tile):
        value = parts_ref[x, tile].astype(F32)
        for z in range(1, sources // NX):
            value = value + parts_ref[z * NX + x, tile].astype(F32)
        return value

    along = total(0, feats)
    for x in range(1, NX):
        along = along + total(x, feats)
    along = jnp.sum(along, axis=1, keepdims=True)
    at = pl.multiple_of(where_ref[6] * 8, 8)
    r = r_ref[pl.ds(at, 8), :][:, :1]
    own = table_ref[...].astype(F32) * (along * (r * r * r) * (1.0 / width))
    for x in range(NX):
        for f in range(feats):
            c = (x * feats + f) * L
            t_ref[0, :, c : c + L] = total(x, f) - own[:, c : c + L]
        gains = total(x, feats + 1) + total(x, feats + 4)
        for f in range(feats):
            c = (x * feats + f) * L
            g_ref[0:1, c : c + L] = gains[f : f + 1]
        h_ref[x * 16 : x * 16 + 8, :] = total(x, feats + 2) + total(x, feats + 5)
        h_ref[x * 16 + 8 : x * 16 + 16, :] = total(x, feats + 3) + total(x, feats + 6)
    b_ref[0] = h_ref[...].T[:32]


def finish(where, parts, table, r):
    width = table.shape[1]
    smem, vmem = pl.BlockSpec(memory_space=pltpu.SMEM), pl.BlockSpec(memory_space=pltpu.VMEM)
    return pl.pallas_call(
        last_kernel,
        in_specs=[smem, vmem, vmem, vmem],
        out_specs=[vmem] * 3,
        out_shape=[
            jax.ShapeDtypeStruct((1, 8, width), F32),
            jax.ShapeDtypeStruct((1, width), F32),
            jax.ShapeDtypeStruct((1, 32, 64), F32),
        ],
        scratch_shapes=[pltpu.VMEM((64, L), F32)],
        compiler_params=pltpu.CompilerParams(vmem_limit_bytes=BIG),
        cost_estimate=pl.CostEstimate(flops=1 << 20, bytes_accessed=2 << 20, transcendentals=0),
        name="finish",
    )(where, parts, table, r)


def local(picks, token_ids, segment_ids, row_order, embed_table, norm_gain, position_bias, returned_grad):
    x, z, c = lax.axis_index("x"), lax.axis_index("z"), lax.axis_index("c")
    table, gain, pos, grad = embed_table[0], norm_gain, position_bias[0], returned_grad[0]
    part = table.shape[1] // NX
    sections = lax.axis_size("section")
    slots = [lax.rem(x + NX - s, NX) for s in range(NX)]
    me = (z * NX + x) * 2 + c
    where = jnp.stack([x] + [(z * NX + k) * 2 + c for k in slots] + [c, me]).astype(jnp.int32)

    def send(value, steps, along):
        pairs = [
            (i * sections + j, (i + steps) % NX * sections + (j + along) % sections)
            for i in range(NX)
            for j in range(sections)
        ]
        return lax.ppermute(value, ("x", "section"), pairs)

    grads = [
        send(lax.dynamic_slice(grad, (0, lax.rem(x + s, NX) * part), (L, part)), s, -1) for s in range(NX)
    ]

    ne, r, bvec = prepare(x[None], table, gain, pos, picks)
    count = 64
    note = jnp.concatenate([token_ids[0], segment_ids[0], jnp.broadcast_to(row_order, (1, L))], axis=0)
    notes = lax.all_to_all(jnp.broadcast_to(note[None], (count, 3, L)), ("z", "x", "c"), 0, 0)
    ids, segs, order = notes[:, 0], notes[:, 1], notes[:, 2, 0]

    *acts, normed, probs = forward(where, order, ids, segs, ne, bvec)
    pieces = [send(acts[s], -s, 1) for s in range(NX)]
    handed = jnp.zeros((L, NX * part), BF16)
    for s in range(NX):
        handed = lax.dynamic_update_slice(handed, pieces[s], (0, lax.rem(x + s, NX) * part))

    own_gain = lax.dynamic_slice(gain, (0, x * part), (1, part))
    wide_picks = jnp.concatenate([picks, jnp.zeros((L - picks.shape[0], L), F32)], axis=0)
    mine, other = backward(where, order, ids, ne, r, own_gain, wide_picks, normed, probs, grads)
    came = lax.ppermute(other, "c", [(0, 1), (1, 0)])
    parts = lax.all_to_all(join(mine, came), ("z", "x"), 0, 0)
    rows = lax.dynamic_slice(table, (me * 8, 0), (8, table.shape[1]))
    return (handed[None],) + tuple(finish(where, parts, rows, r))


def solution(mesh):
    fine = Mesh(mesh.devices.reshape(8, NX, 2, 4), ("z", "x", "c", "section"))
    dp = ("z", "x", "c")
    placed = (
        P(),
        P("section", dp, None),
        P("section", dp, None),
        P("section", dp),
        P("section", None, None),
        P("section", None),
        P("section", None, None),
        P("section", dp, None),
    )
    mapped = jax.shard_map(
        local,
        mesh=fine,
        in_specs=placed,
        out_specs=(
            P("section", dp, None),
            P("section", dp, None),
            P("section", None),
            P("section", None, None),
        ),
        check_vma=False,
    )
    return lambda *args: mapped(jnp.asarray(bucket_picks()), *args)
```

```python
import functools

import jax
import jax.numpy as jnp
import numpy as np
from jax import lax
from jax.experimental import pallas as pl
from jax.experimental.pallas import tpu as pltpu
from jax.sharding import Mesh, PartitionSpec as P

F32, BF16 = jnp.float32, jnp.bfloat16
LIMITS = (12, 16, 23, 32, 45, 64, 91)
LOG2E = 1.4426950408889634
L = 128
NX = 4
MIB = 1024 * 1024


def bucket_picks():
    c = np.arange(L)
    r = -np.where(c < 64, c, c - L)
    a = np.abs(r)
    b = np.minimum(a, 8) + sum((a >= t).astype(np.int64) for t in LIMITS) + 16 * (r > 0)
    return (np.arange(L)[:, None] == b[None, :]).astype(np.float32)


def dot(a, b, dims, precision=None):
    return lax.dot_general(a, b, (dims, ((), ())), precision=precision, preferred_element_type=F32)


NN, NT, TN = ((1,), (0,)), ((1,), (1,)), ((0,), (0,))


def halves(tile):
    low = lax.broadcasted_iota(jnp.int32, tile.shape, 1) < 64
    zero = jnp.zeros_like(tile)
    return jnp.concatenate([jnp.where(low, tile, zero), jnp.where(low, zero, tile)], axis=0)


def offset_sums(square):
    acc = square[:8]
    for k in range(8, L, 8):
        acc = acc + pltpu.roll(square[k : k + 8], L - k, 1)
    row = lax.broadcasted_iota(jnp.int32, acc.shape, 0)
    for bit in (1, 2, 4):
        acc = jnp.where((row & bit) != 0, pltpu.roll(acc, L - bit, 1), acc)
    return jnp.sum(acc, axis=0, keepdims=True)


def cost(us, mib):
    return pl.CostEstimate(flops=int(us * 1e9), bytes_accessed=int(mib * MIB), transcendentals=0)


def place():
    return lax.axis_index("z"), lax.axis_index("x"), lax.axis_index("c")


def pre_kernel(table_ref, gain_ref, pos_ref, picks_ref, ne_ref, r_ref, bvec_ref):
    width = table_ref.shape[1]
    part = width // NX
    wide = table_ref[...].astype(F32)
    r = lax.rsqrt(jnp.sum(wide * wide, axis=1, keepdims=True) * (1.0 / width) + 1e-06)
    r_ref[...] = jnp.broadcast_to(r, r_ref.shape)
    cols = pl.ds(pl.multiple_of(lax.axis_index("x") * part, L), part)
    own = table_ref[:, cols]
    ne_ref[:, :part] = (own.astype(F32) * r * gain_ref[:, cols]).astype(BF16)
    ne_ref[:, part:] = own

    @pl.when(pl.program_id(0) == 0)
    def _():
        bvec_ref[...] = dot(pos_ref[...], picks_ref[...], TN, lax.Precision.HIGHEST) * LOG2E


def prepare(table, gain, pos, picks):
    vocab, width = table.shape
    part = width // NX
    rows = 128
    heads = pos.shape[1]
    return pl.pallas_call(
        pre_kernel,
        grid=(vocab // rows,),
        in_specs=[
            pl.BlockSpec((rows, width), lambda i: (i, 0)),
            pl.BlockSpec((1, width), lambda i: (0, 0)),
            pl.BlockSpec(pos.shape, lambda i: (0, 0)),
            pl.BlockSpec(picks.shape, lambda i: (0, 0)),
        ],
        out_specs=[
            pl.BlockSpec((rows, 2 * part), lambda i: (i, 0)),
            pl.BlockSpec((rows, L), lambda i: (i, 0)),
            pl.BlockSpec((heads, L), lambda i: (0, 0)),
        ],
        out_shape=[
            jax.ShapeDtypeStruct((vocab, 2 * part), BF16),
            jax.ShapeDtypeStruct((vocab, L), F32),
            jax.ShapeDtypeStruct((heads, L), F32),
        ],
        compiler_params=pltpu.CompilerParams(vmem_limit_bytes=12 * MIB),
        cost_estimate=cost(5, 7),
        name="prepare",
    )(table, gain, pos, picks)


def onehot_t(ids_row, vocab):
    v = lax.broadcasted_iota(jnp.int32, (vocab, ids_row.shape[1]), 0)
    return jnp.where(v == ids_row, 1.0, 0.0).astype(BF16)


def packed(notes_ref, slot, what):
    z, x, c = place()
    chip = z * NX + lax.rem(x + NX - slot, NX)
    order = notes_ref[pl.ds(chip * 2 + c, 1), 2, :]
    values = notes_ref[:, what, :]
    found = lax.broadcasted_iota(jnp.int32, values.shape, 0) == order
    return jnp.sum(jnp.where(found, values, 0), axis=0, keepdims=True)


def fwd_kernel(notes_ref, ne_ref, bvec_ref, *rest):
    a_refs, (n_ref, p_ref), (e_ref, m_ref) = rest[:NX], rest[NX : NX + 2], rest[NX + 2 :]
    vocab, part = ne_ref.shape[0], ne_ref.shape[1] // 2
    pairs = part // L
    first = lax.axis_index("x") * (2 * pairs)
    for s in range(NX):
        both = dot(onehot_t(packed(notes_ref, s, 0), vocab), ne_ref[...], TN)
        n_ref[s] = both[:, :part].astype(BF16)
        e_ref[s] = both[:, part:].astype(BF16)
        seg = jnp.broadcast_to(packed(notes_ref, s, 1), (L, L)).astype(F32)
        m_ref[s] = jnp.where(seg == seg.T, 0.0, -1e30)

    @pl.loop(0, pairs)
    def _(p):
        cols = pl.ds(pl.multiple_of(p * L, L), L)
        biases = [
            pltpu.roll(
                jnp.broadcast_to(bvec_ref[pl.ds(first + 2 * p + k, 1), :], (L, L)),
                0,
                1,
                stride=1,
                stride_axis=0,
            )
            for k in range(2)
        ]
        for s in range(NX):
            tile = n_ref[s, :, cols]
            two = halves(tile)
            mask = m_ref[s]
            raw = dot(two, tile, NT)
            for k in range(2):
                scores = raw[k * L : (k + 1) * L] * (LOG2E / 64.0) + (biases[k] + mask)
                expo = jnp.exp2(scores - jnp.max(scores, axis=0, keepdims=True))
                probs = expo * (1.0 / jnp.sum(expo, axis=0, keepdims=True))
                p_ref[p, s, k * L : (k + 1) * L] = probs.astype(BF16)
            mixed = dot(p_ref[p, s], two, TN)
            a_refs[s][:, cols] = (e_ref[s, :, cols].astype(F32) + mixed).astype(BF16)


def forward(notes, ne, bvec):
    part = ne.shape[1] // 2
    pairs = part // L
    vmem = pl.BlockSpec(memory_space=pltpu.VMEM)
    return pl.pallas_call(
        fwd_kernel,
        in_specs=[vmem] * 3,
        out_specs=[vmem] * (NX + 2),
        out_shape=[jax.ShapeDtypeStruct((L, part), BF16)] * NX
        + [
            jax.ShapeDtypeStruct((NX, L, part), BF16),
            jax.ShapeDtypeStruct((pairs, NX, 2 * L, L), BF16),
        ],
        scratch_shapes=[pltpu.VMEM((NX, L, part), BF16), pltpu.VMEM((NX, L, L), F32)],
        compiler_params=pltpu.CompilerParams(vmem_limit_bytes=18 * MIB),
        cost_estimate=cost(8, 7),
        name="forward",
    )(notes, ne, bvec)


def bwd_kernel(notes_ref, ne_ref, r_ref, gain_ref, picks_ref, n_ref, p_ref, *rest):
    g_refs, (mine_ref, other_ref), (d_ref, rg_ref, o_ref, diag_ref) = rest[:NX], rest[NX : NX + 2], rest[NX + 2 :]
    vocab, part = ne_ref.shape[0], ne_ref.shape[1] // 2
    pairs = part // L
    blocks = vocab // 16
    _, x, core = place()

    @pl.loop(0, pairs)
    def _(p):
        cols = pl.ds(pl.multiple_of(p * L, L), L)
        total = [jnp.zeros((L, L), F32)] * 2
        for s in range(NX):
            tile, up = n_ref[s, :, cols], g_refs[s][:, cols]
            rg_ref[pl.ds(s * L, L), cols] = up
            two, ups = halves(tile), halves(up)
            d_all = dot(two, up, NT)
            small = []
            for k in range(2):
                wide = p_ref[p, s, k * L : (k + 1) * L].astype(F32)
                d_probs = d_all[k * L : (k + 1) * L].astype(BF16).astype(F32)
                d_scores = wide * (d_probs - jnp.sum(wide * d_probs, axis=0, keepdims=True))
                total[k] = total[k] + d_scores
                small.append(d_scores.astype(BF16))
            part64 = two * BF16(1.0 / 64.0)
            left = jnp.concatenate([p_ref[p, s, :L], p_ref[p, s, L:]] + small, axis=1)
            d_norm = dot(left, jnp.concatenate([ups, part64], axis=0), NN)
            d_norm = d_norm + dot(jnp.concatenate(small, axis=0), part64, TN)
            d_ref[pl.ds(s * L, L), cols] = d_norm.astype(BF16)
        for k in range(2):
            diag_ref[pl.ds(2 * p + k, 1), :] = offset_sums(total[k])

    for s in range(NX):
        o_ref[:, s * L : (s + 1) * L] = onehot_t(packed(notes_ref, s, 0), vocab)

    def put(tile, value):
        value = value.reshape(blocks, 2, 8, L)
        first, second = value[:, 0], value[:, 1]
        mine_ref[0:blocks, tile] = jnp.where(core == 0, first, second)
        other_ref[0:blocks, tile] = jnp.where(core == 0, second, first)

    r = r_ref[...]
    along = jnp.zeros((vocab, L), F32)
    for f in range(pairs):
        cols = slice(f * L, (f + 1) * L)
        d_act = dot(o_ref[...], rg_ref[:, cols], NN)
        d_norm = dot(o_ref[...], d_ref[:, cols], NN)
        gain = gain_ref[:, pl.ds(pl.multiple_of(x * part + f * L, L), L)]
        own = ne_ref[:, part + f * L : part + (f + 1) * L].astype(F32)
        scaled = d_norm * r
        put(f, d_act + scaled * gain)
        along = along + own * (d_norm * gain)
        g_row = jnp.sum(own * scaled, axis=0, keepdims=True)
        mine_ref[blocks, 0, pl.ds(f, 1), :] = g_row
        other_ref[blocks, 0, pl.ds(f, 1), :] = g_row
    put(pairs, along)
    sums = dot(diag_ref[...], picks_ref[...], NT, lax.Precision.HIGHEST)
    for ref in (mine_ref, other_ref):
        ref[blocks, 1] = sums[:8]
        ref[blocks, 2] = sums[8:]
        for tile in range(3, pairs + 1):
            ref[blocks, tile] = jnp.zeros((8, L), F32)


def backward(notes, ne, r, gain, picks, n, probs, grads):
    vocab, part = ne.shape[0], ne.shape[1] // 2
    pairs = part // L
    vmem = pl.BlockSpec(memory_space=pltpu.VMEM)
    out = jax.ShapeDtypeStruct((vocab // 16 + 1, pairs + 1, 8, L), F32)
    return pl.pallas_call(
        bwd_kernel,
        in_specs=[vmem] * (7 + NX),
        out_specs=[vmem, vmem],
        out_shape=[out, out],
        scratch_shapes=[
            pltpu.VMEM((NX * L, part), BF16),
            pltpu.VMEM((NX * L, part), BF16),
            pltpu.VMEM((vocab, NX * L), BF16),
            pltpu.VMEM((2 * pairs, L), F32),
        ],
        compiler_params=pltpu.CompilerParams(vmem_limit_bytes=24 * MIB),
        cost_estimate=cost(10, 10),
        name="backward",
    )(notes, ne, r, gain, picks, n, probs, *grads)


def join_kernel(mine_ref, came_ref, out_ref):
    blocks, tiles = mine_ref.shape[0] - 1, mine_ref.shape[1] - 1
    for t in range(tiles):
        out_ref[:, t] = (mine_ref[0:blocks, t] + came_ref[0:blocks, t]).astype(BF16)
    sums = [mine_ref[blocks, t] + came_ref[blocks, t] for t in range(3)]
    out_ref[:, tiles] = jnp.broadcast_to(sums[0].astype(BF16)[None], (blocks, 8, L))
    bias = sums[1] + pltpu.roll(sums[2], 32, 1)
    lane = lax.broadcasted_iota(jnp.int32, (8, L), 1)
    for d in range(blocks):
        along = jnp.sum(mine_ref[d, tiles] + came_ref[d, tiles], axis=1, keepdims=True)
        value = jnp.where(lane == 16, along, bias)
        high = value.astype(BF16).astype(F32)
        out_ref[d, tiles + 1] = (high + pltpu.roll(value - high, 64, 1)).astype(BF16)


def join(mine, came):
    blocks, tiles = mine.shape[0] - 1, mine.shape[1]
    vmem = pl.BlockSpec(memory_space=pltpu.VMEM)
    return pl.pallas_call(
        join_kernel,
        in_specs=[vmem, vmem],
        out_specs=vmem,
        out_shape=jax.ShapeDtypeStruct((blocks, tiles + 1, 8, L), BF16),
        compiler_params=pltpu.CompilerParams(vmem_limit_bytes=8 * MIB),
        cost_estimate=cost(2, 4),
        name="join",
    )(mine, came)


def last_kernel(parts_ref, table_ref, r_ref, t_ref, g_ref, b_ref, h_ref):
    sources, feats = parts_ref.shape[0], parts_ref.shape[1] - 2
    width = table_ref.shape[1]
    z, x_own, c = place()
    lane = lax.broadcasted_iota(jnp.int32, (8, L), 1)

    def total(x, tile):
        value = parts_ref[x, tile].astype(F32)
        for k in range(1, sources // NX):
            value = value + parts_ref[k * NX + x, tile].astype(F32)
        return value

    along = jnp.zeros((8, 1), F32)
    for x in range(NX):
        value = total(x, feats + 1)
        value = value + pltpu.roll(value, 64, 1)
        along = along + jnp.sum(jnp.where(lane == 16, value, 0.0), axis=1, keepdims=True)
        value = jnp.where(lane == 16, 0.0, value)
        h_ref[x * 16 : x * 16 + 8, :] = value
        h_ref[x * 16 + 8 : x * 16 + 16, :] = pltpu.roll(value, L - 32, 1)
    b_ref[0] = h_ref[...].T[:32]
    at = pl.multiple_of(((z * NX + x_own) * 2 + c) * 8, 8)
    r = r_ref[pl.ds(at, 8), :][:, :1]
    factor = along * (r * r * r) * (1.0 / width)
    for x in range(NX):
        gains = total(x, feats)
        for f in range(feats):
            k = (x * feats + f) * L
            t_ref[0, :, k : k + L] = total(x, f) - table_ref[:, k : k + L].astype(F32) * factor
            g_ref[0:1, k : k + L] = gains[f : f + 1]


def finish(parts, table, r):
    width = table.shape[1]
    vmem = pl.BlockSpec(memory_space=pltpu.VMEM)
    return pl.pallas_call(
        last_kernel,
        in_specs=[vmem, vmem, vmem],
        out_specs=[vmem] * 3,
        out_shape=[
            jax.ShapeDtypeStruct((1, 8, width), F32),
            jax.ShapeDtypeStruct((1, width), F32),
            jax.ShapeDtypeStruct((1, 32, 64), F32),
        ],
        scratch_shapes=[pltpu.VMEM((64, L), F32)],
        compiler_params=pltpu.CompilerParams(vmem_limit_bytes=8 * MIB),
        cost_estimate=cost(2, 2),
        name="finish",
    )(parts, table, r)


def local(picks, token_ids, segment_ids, row_order, embed_table, norm_gain, position_bias, returned_grad):
    x, z, c = lax.axis_index("x"), lax.axis_index("z"), lax.axis_index("c")
    table, gain, pos, grad = embed_table[0], norm_gain, position_bias[0], returned_grad[0]
    part = table.shape[1] // NX
    sections = lax.axis_size("section")

    def send(value, steps, along):
        pairs = [
            (i * sections + j, (i + steps) % NX * sections + (j + along) % sections)
            for i in range(NX)
            for j in range(sections)
        ]
        return lax.ppermute(value, ("x", "section"), pairs)

    grads = [
        send(lax.dynamic_slice(grad, (0, lax.rem(x + s, NX) * part), (L, part)), s, -1) for s in range(NX)
    ]

    ne, r, bvec = prepare(table, gain, pos, picks[:32])
    count = 64
    note = jnp.concatenate([token_ids[0], segment_ids[0], jnp.broadcast_to(row_order, (1, L))], axis=0)
    notes = lax.all_to_all(jnp.broadcast_to(note[None], (count, 3, L)), ("z", "x", "c"), 0, 0)

    *acts, normed, probs = forward(notes, ne, bvec)
    pieces = [send(acts[s], -s, 1) for s in range(NX)]
    handed = jnp.zeros((L, NX * part), BF16)
    for s in range(NX):
        handed = lax.dynamic_update_slice(handed, pieces[s], (0, lax.rem(x + s, NX) * part))

    mine, other = backward(notes, ne, r, gain, picks, normed, probs, grads)
    came = lax.ppermute(other, "c", [(0, 1), (1, 0)])
    parts = lax.all_to_all(join(mine, came), ("z", "x"), 0, 0)
    rows = lax.dynamic_slice(table, (((z * NX + x) * 2 + c) * 8, 0), (8, table.shape[1]))
    return (handed[None],) + tuple(finish(parts, rows, r))


def solution(mesh):
    fine = Mesh(mesh.devices.reshape(8, NX, 2, 4), ("z", "x", "c", "section"))
    dp = ("z", "x", "c")
    placed = (
        P(),
        P("section", dp, None),
        P("section", dp, None),
        P("section", dp),
        P("section", None, None),
        P("section", None),
        P("section", None, None),
        P("section", dp, None),
    )
    mapped = jax.shard_map(
        local,
        mesh=fine,
        in_specs=placed,
        out_specs=(
            P("section", dp, None),
            P("section", dp, None),
            P("section", None),
            P("section", None, None),
        ),
        check_vma=False,
    )
    return lambda *args: mapped(jnp.asarray(bucket_picks()), *args)
```

```python
import functools

import jax
import jax.numpy as jnp
import numpy as np
from jax import lax
from jax.experimental import pallas as pl
from jax.experimental.pallas import tpu as pltpu
from jax.sharding import Mesh, PartitionSpec as P

F32, BF16 = jnp.float32, jnp.bfloat16
LIMITS = (12, 16, 23, 32, 45, 64, 91)
LOG2E = 1.4426950408889634
L = 128
NX = 4
MIB = 1024 * 1024


def bucket_picks():
    c = np.arange(L)
    r = -np.where(c < 64, c, c - L)
    a = np.abs(r)
    b = np.minimum(a, 8) + sum((a >= t).astype(np.int64) for t in LIMITS) + 16 * (r > 0)
    return (np.arange(L)[:, None] == b[None, :]).astype(np.float32)


def dot(a, b, dims, precision=None):
    return lax.dot_general(a, b, (dims, ((), ())), precision=precision, preferred_element_type=F32)


NN, NT, TN = ((1,), (0,)), ((1,), (1,)), ((0,), (0,))


def halves(tile):
    low = lax.broadcasted_iota(jnp.int32, tile.shape, 1) < 64
    zero = jnp.zeros_like(tile)
    return jnp.concatenate([jnp.where(low, tile, zero), jnp.where(low, zero, tile)], axis=0)


def offset_sums(square):
    acc = square[:8]
    for k in range(8, L, 8):
        acc = acc + pltpu.roll(square[k : k + 8], L - k, 1)
    row = lax.broadcasted_iota(jnp.int32, acc.shape, 0)
    for bit in (1, 2, 4):
        acc = jnp.where((row & bit) != 0, pltpu.roll(acc, L - bit, 1), acc)
    return jnp.sum(acc, axis=0, keepdims=True)


def cost(us, mib):
    return pl.CostEstimate(flops=int(us * 1e9), bytes_accessed=int(mib * MIB), transcendentals=0)


def place():
    return lax.axis_index("z"), lax.axis_index("x"), lax.axis_index("c")


def pre_kernel(table_ref, gain_ref, pos_ref, picks_ref, ne_ref, r_ref, bvec_ref):
    width = table_ref.shape[1]
    part = width // NX
    wide = table_ref[...].astype(F32)
    r = lax.rsqrt(jnp.sum(wide * wide, axis=1, keepdims=True) * (1.0 / width) + 1e-06)
    r_ref[...] = jnp.broadcast_to(r, r_ref.shape)
    cols = pl.ds(pl.multiple_of(lax.axis_index("x") * part, L), part)
    own = table_ref[:, cols]
    ne_ref[:, :part] = (own.astype(F32) * r * gain_ref[:, cols]).astype(BF16)
    ne_ref[:, part:] = own

    @pl.when(pl.program_id(0) == 0)
    def _():
        bvec_ref[...] = dot(pos_ref[...], picks_ref[...], TN, lax.Precision.HIGHEST) * LOG2E


def prepare(table, gain, pos, picks):
    vocab, width = table.shape
    part = width // NX
    rows = 128
    heads = pos.shape[1]
    return pl.pallas_call(
        pre_kernel,
        grid=(vocab // rows,),
        in_specs=[
            pl.BlockSpec((rows, width), lambda i: (i, 0)),
            pl.BlockSpec((1, width), lambda i: (0, 0)),
            pl.BlockSpec(pos.shape, lambda i: (0, 0)),
            pl.BlockSpec(picks.shape, lambda i: (0, 0)),
        ],
        out_specs=[
            pl.BlockSpec((rows, 2 * part), lambda i: (i, 0)),
            pl.BlockSpec((rows, L), lambda i: (i, 0)),
            pl.BlockSpec((heads, L), lambda i: (0, 0)),
        ],
        out_shape=[
            jax.ShapeDtypeStruct((vocab, 2 * part), BF16),
            jax.ShapeDtypeStruct((vocab, L), F32),
            jax.ShapeDtypeStruct((heads, L), F32),
        ],
        compiler_params=pltpu.CompilerParams(vmem_limit_bytes=12 * MIB),
        cost_estimate=cost(5, 7),
        name="prepare",
    )(table, gain, pos, picks)


def onehot_t(ids_row, vocab):
    v = lax.broadcasted_iota(jnp.int32, (vocab, ids_row.shape[1]), 0)
    return jnp.where(v == ids_row, 1.0, 0.0).astype(BF16)


def packed(notes_ref, slot, what):
    z, x, c = place()
    chip = z * NX + lax.rem(x + NX - slot, NX)
    order = notes_ref[pl.ds(chip * 2 + c, 1), 2, :]
    values = notes_ref[:, what, :]
    found = lax.broadcasted_iota(jnp.int32, values.shape, 0) == order
    return jnp.sum(jnp.where(found, values, 0), axis=0, keepdims=True)


def fwd_kernel(notes_ref, ne_hbm, bvec_hbm, *rest):
    a_refs, (n_ref, p_ref), (e_ref, m_ref, ne_ref, bvec_ref, sems) = rest[:NX], rest[NX : NX + 2], rest[NX + 2 :]
    eighth = ne_ref.shape[0] // 8
    copies = [
        pltpu.make_async_copy(ne_hbm.at[pl.ds(k * eighth, eighth)], ne_ref.at[pl.ds(k * eighth, eighth)], sems.at[k])
        for k in range(8)
    ]
    copies.append(pltpu.make_async_copy(bvec_hbm, bvec_ref, sems.at[8]))
    for copy in copies:
        copy.start()
    vocab, part = ne_ref.shape[0], ne_ref.shape[1] // 2
    pairs = part // L
    first = lax.axis_index("x") * (2 * pairs)
    for s in range(NX):
        seg = jnp.broadcast_to(packed(notes_ref, s, 1), (L, L)).astype(F32)
        m_ref[s] = jnp.where(seg == seg.T, 0.0, -1e30)
    picked = [onehot_t(packed(notes_ref, s, 0), vocab) for s in range(NX)]
    for copy in copies:
        copy.wait()
    for s in range(NX):
        both = dot(picked[s], ne_ref[...], TN)
        n_ref[s] = both[:, :part].astype(BF16)
        e_ref[s] = both[:, part:].astype(BF16)

    @pl.loop(0, pairs)
    def _(p):
        cols = pl.ds(pl.multiple_of(p * L, L), L)
        biases = [
            pltpu.roll(
                jnp.broadcast_to(bvec_ref[pl.ds(first + 2 * p + k, 1), :], (L, L)),
                0,
                1,
                stride=1,
                stride_axis=0,
            )
            for k in range(2)
        ]
        for s in range(NX):
            tile = n_ref[s, :, cols]
            two = halves(tile)
            mask = m_ref[s]
            raw = dot(two, tile, NT)
            for k in range(2):
                scores = raw[k * L : (k + 1) * L] * (LOG2E / 64.0) + (biases[k] + mask)
                expo = jnp.exp2(scores - jnp.max(scores, axis=0, keepdims=True))
                probs = expo * (1.0 / jnp.sum(expo, axis=0, keepdims=True))
                p_ref[p, s, k * L : (k + 1) * L] = probs.astype(BF16)
            mixed = dot(p_ref[p, s], two, TN)
            a_refs[s][:, cols] = (e_ref[s, :, cols].astype(F32) + mixed).astype(BF16)


def forward(notes, ne, bvec):
    part = ne.shape[1] // 2
    pairs = part // L
    vmem, hbm = pl.BlockSpec(memory_space=pltpu.VMEM), pl.BlockSpec(memory_space=pltpu.HBM)
    return pl.pallas_call(
        fwd_kernel,
        in_specs=[vmem, hbm, hbm],
        out_specs=[vmem] * (NX + 2),
        out_shape=[jax.ShapeDtypeStruct((L, part), BF16)] * NX
        + [
            jax.ShapeDtypeStruct((NX, L, part), BF16),
            jax.ShapeDtypeStruct((pairs, NX, 2 * L, L), BF16),
        ],
        scratch_shapes=[
            pltpu.VMEM((NX, L, part), BF16),
            pltpu.VMEM((NX, L, L), F32),
            pltpu.VMEM(ne.shape, BF16),
            pltpu.VMEM(bvec.shape, F32),
            pltpu.SemaphoreType.DMA((9,)),
        ],
        compiler_params=pltpu.CompilerParams(vmem_limit_bytes=18 * MIB),
        cost_estimate=cost(8, 7),
        name="forward",
    )(notes, ne, bvec)


def bwd_kernel(notes_ref, ne_ref, r_ref, gain_ref, picks_ref, n_ref, p_ref, *rest):
    g_refs, (mine_ref, other_ref), rest = rest[:NX], rest[NX : NX + 2], rest[NX + 2 :]
    d_ref, rg_ref, o_ref, diag_ref = rest
    vocab, part = ne_ref.shape[0], ne_ref.shape[1] // 2
    pairs = part // L
    blocks = vocab // 16
    _, x, core = place()

    @pl.loop(0, pairs)
    def _(p):
        cols = pl.ds(pl.multiple_of(p * L, L), L)
        total = [jnp.zeros((L, L), F32)] * 2
        for s in range(NX):
            tile, up = n_ref[s, :, cols], g_refs[s][:, cols]
            rg_ref[pl.ds(s * L, L), cols] = up
            two, ups = halves(tile), halves(up)
            d_all = dot(two, up, NT)
            small = []
            for k in range(2):
                wide = p_ref[p, s, k * L : (k + 1) * L].astype(F32)
                d_probs = d_all[k * L : (k + 1) * L].astype(BF16).astype(F32)
                d_scores = wide * (d_probs - jnp.sum(wide * d_probs, axis=0, keepdims=True))
                total[k] = total[k] + d_scores
                small.append(d_scores.astype(BF16))
            part64 = two * BF16(1.0 / 64.0)
            left = jnp.concatenate([p_ref[p, s, :L], p_ref[p, s, L:]] + small, axis=1)
            d_norm = dot(left, jnp.concatenate([ups, part64], axis=0), NN)
            d_norm = d_norm + dot(jnp.concatenate(small, axis=0), part64, TN)
            d_ref[pl.ds(s * L, L), cols] = d_norm.astype(BF16)
        for k in range(2):
            diag_ref[pl.ds(2 * p + k, 1), :] = offset_sums(total[k])

    for s in range(NX):
        o_ref[:, s * L : (s + 1) * L] = onehot_t(packed(notes_ref, s, 0), vocab)

    def put(tile, value):
        value = value.reshape(blocks, 2, 8, L)
        first, second = value[:, 0], value[:, 1]
        mine_ref[tile] = jnp.where(core == 0, first, second)
        other_ref[tile] = jnp.where(core == 0, second, first)

    r = r_ref[...]
    along = jnp.zeros((vocab, L), F32)
    for f in range(pairs):
        cols = slice(f * L, (f + 1) * L)
        d_act = dot(o_ref[...], rg_ref[:, cols], NN)
        d_norm = dot(o_ref[...], d_ref[:, cols], NN)
        gain = gain_ref[:, pl.ds(pl.multiple_of(x * part + f * L, L), L)]
        own = ne_ref[:, part + f * L : part + (f + 1) * L].astype(F32)
        scaled = d_norm * r
        put(f, d_act + scaled * gain)
        along = along + own * (d_norm * gain)
        g_row = jnp.sum(own * scaled, axis=0, keepdims=True)
        for ref in (mine_ref, other_ref):
            ref[pairs + 1, 0, pl.ds(f, 1), :] = g_row
    put(pairs, along)
    sums = dot(diag_ref[...], picks_ref[...], NT, lax.Precision.HIGHEST)
    for ref in (mine_ref, other_ref):
        ref[pairs + 1, 1] = sums[:8]
        ref[pairs + 1, 2] = sums[8:]
        ref[pairs + 1, 3:] = jnp.zeros((blocks - 3, 8, L), F32)


def backward(notes, ne, r, gain, picks, n, probs, grads):
    vocab, part = ne.shape[0], ne.shape[1] // 2
    pairs = part // L
    vmem = pl.BlockSpec(memory_space=pltpu.VMEM)
    stacked = (pairs + 2, vocab // 16, 8, L)
    out = jax.ShapeDtypeStruct(stacked, F32)
    return pl.pallas_call(
        bwd_kernel,
        in_specs=[vmem] * (7 + NX),
        out_specs=[vmem, vmem],
        out_shape=[out, out],
        scratch_shapes=[
            pltpu.VMEM((NX * L, part), BF16),
            pltpu.VMEM((NX * L, part), BF16),
            pltpu.VMEM((vocab, NX * L), BF16),
            pltpu.VMEM((2 * pairs, L), F32),
        ],
        compiler_params=pltpu.CompilerParams(vmem_limit_bytes=24 * MIB),
        cost_estimate=cost(10, 10),
        name="backward",
    )(notes, ne, r, gain, picks, n, probs, *grads)


def join_kernel(mine_ref, came_ref, out_ref):
    tiles, blocks = mine_ref.shape[0] - 2, mine_ref.shape[1]
    for t in range(tiles):
        out_ref[:, t] = (mine_ref[t] + came_ref[t]).astype(BF16)
    sums = [mine_ref[tiles + 1, t] + came_ref[tiles + 1, t] for t in range(3)]
    out_ref[:, tiles] = jnp.broadcast_to(sums[0].astype(BF16)[None], (blocks, 8, L))
    bias = sums[1] + pltpu.roll(sums[2], 32, 1)
    lane = lax.broadcasted_iota(jnp.int32, (8, L), 1)
    for d in range(blocks):
        along = jnp.sum(mine_ref[tiles, d] + came_ref[tiles, d], axis=1, keepdims=True)
        value = jnp.where(lane == 16, along, bias)
        high = value.astype(BF16).astype(F32)
        out_ref[d, tiles + 1] = (high + pltpu.roll(value - high, 64, 1)).astype(BF16)


def join(mine, came):
    tiles, blocks = mine.shape[:2]
    vmem = pl.BlockSpec(memory_space=pltpu.VMEM)
    return pl.pallas_call(
        join_kernel,
        in_specs=[vmem, vmem],
        out_specs=vmem,
        out_shape=jax.ShapeDtypeStruct((blocks, tiles, 8, L), BF16),
        compiler_params=pltpu.CompilerParams(vmem_limit_bytes=8 * MIB),
        cost_estimate=cost(2, 4),
        name="join",
    )(mine, came)


def last_kernel(parts_ref, table_ref, r_ref, t_ref, g_ref, b_ref, h_ref):
    sources, feats = parts_ref.shape[0], parts_ref.shape[1] - 2
    width = table_ref.shape[1]
    z, x_own, c = place()
    lane = lax.broadcasted_iota(jnp.int32, (8, L), 1)

    def total(x, tile):
        value = parts_ref[x, tile].astype(F32)
        for k in range(1, sources // NX):
            value = value + parts_ref[k * NX + x, tile].astype(F32)
        return value

    along = jnp.zeros((8, 1), F32)
    for x in range(NX):
        value = total(x, feats + 1)
        value = value + pltpu.roll(value, 64, 1)
        along = along + jnp.sum(jnp.where(lane == 16, value, 0.0), axis=1, keepdims=True)
        value = jnp.where(lane == 16, 0.0, value)
        h_ref[x * 16 : x * 16 + 8, :] = value
        h_ref[x * 16 + 8 : x * 16 + 16, :] = pltpu.roll(value, L - 32, 1)
    b_ref[0] = h_ref[...].T[:32]
    at = pl.multiple_of(((z * NX + x_own) * 2 + c) * 8, 8)
    r = r_ref[pl.ds(at, 8), :][:, :1]
    factor = along * (r * r * r) * (1.0 / width)
    for x in range(NX):
        gains = total(x, feats)
        for f in range(feats):
            k = (x * feats + f) * L
            t_ref[0, :, k : k + L] = total(x, f) - table_ref[:, k : k + L].astype(F32) * factor
            g_ref[0:1, k : k + L] = gains[f : f + 1]


def finish(parts, table, r):
    width = table.shape[1]
    vmem = pl.BlockSpec(memory_space=pltpu.VMEM)
    return pl.pallas_call(
        last_kernel,
        in_specs=[vmem, vmem, vmem],
        out_specs=[vmem] * 3,
        out_shape=[
            jax.ShapeDtypeStruct((1, 8, width), F32),
            jax.ShapeDtypeStruct((1, width), F32),
            jax.ShapeDtypeStruct((1, 32, 64), F32),
        ],
        scratch_shapes=[pltpu.VMEM((64, L), F32)],
        compiler_params=pltpu.CompilerParams(vmem_limit_bytes=8 * MIB),
        cost_estimate=cost(2, 2),
        name="finish",
    )(parts, table, r)


def local(picks, token_ids, segment_ids, row_order, embed_table, norm_gain, position_bias, returned_grad):
    x, z, c = lax.axis_index("x"), lax.axis_index("z"), lax.axis_index("c")
    table, gain, pos, grad = embed_table[0], norm_gain, position_bias[0], returned_grad[0]
    part = table.shape[1] // NX
    sections = lax.axis_size("section")

    def send(value, steps, along):
        pairs = [
            (i * sections + j, (i + steps) % NX * sections + (j + along) % sections)
            for i in range(NX)
            for j in range(sections)
        ]
        return lax.ppermute(value, ("x", "section"), pairs)

    grads = [
        send(lax.dynamic_slice(grad, (0, lax.rem(x + s, NX) * part), (L, part)), s, -1) for s in range(NX)
    ]

    table_then, grads[2] = lax.optimization_barrier((table, grads[2]))
    ne, r, bvec = prepare(table_then, gain, pos, picks[:32])
    count = 64
    note = [jnp.broadcast_to(v.reshape(1, 1, -1), (count, 1, L)) for v in (token_ids, segment_ids, row_order)]
    notes = lax.all_to_all(jnp.concatenate(note, axis=1), ("z", "x", "c"), 0, 0)

    *acts, normed, probs = forward(notes, ne, bvec)
    pieces = {s: send(acts[s], -s, 1) for s in (2, 1, 3, 0)}
    mine, other = backward(notes, ne, r, gain, picks, normed, probs, grads)
    came = lax.ppermute(other, "c", [(0, 1), (1, 0)])
    handed = jnp.zeros((L, NX * part), BF16)
    for s in (2, 1, 3, 0):
        handed = lax.dynamic_update_slice(handed, pieces[s], (0, lax.rem(x + s, NX) * part))

    parts = lax.all_to_all(join(mine, came), ("z", "x"), 0, 0)
    rows = lax.dynamic_slice(table, (((z * NX + x) * 2 + c) * 8, 0), (8, table.shape[1]))
    return (handed[None],) + tuple(finish(parts, rows, r))


def solution(mesh):
    fine = Mesh(mesh.devices.reshape(8, NX, 2, 4), ("z", "x", "c", "section"))
    dp = ("z", "x", "c")
    placed = (
        P(),
        P("section", dp, None),
        P("section", dp, None),
        P("section", dp),
        P("section", None, None),
        P("section", None),
        P("section", None, None),
        P("section", dp, None),
    )
    mapped = jax.shard_map(
        local,
        mesh=fine,
        in_specs=placed,
        out_specs=(
            P("section", dp, None),
            P("section", dp, None),
            P("section", None),
            P("section", None, None),
        ),
        check_vma=False,
    )
    return lambda *args: mapped(jnp.asarray(bucket_picks()), *args)
```

```python
import functools

import jax
import jax.numpy as jnp
import numpy as np
from jax import lax
from jax.experimental import pallas as pl
from jax.experimental.pallas import tpu as pltpu
from jax.sharding import Mesh, PartitionSpec as P

F32, BF16 = jnp.float32, jnp.bfloat16
LIMITS = (12, 16, 23, 32, 45, 64, 91)
UF, UB = 8, 8
LOG2E = 1.4426950408889634
L = 128
NX = 4
MIB = 1024 * 1024


def bucket_picks():
    c = np.arange(L)
    r = -np.where(c < 64, c, c - L)
    a = np.abs(r)
    b = np.minimum(a, 8) + sum((a >= t).astype(np.int64) for t in LIMITS) + 16 * (r > 0)
    return (np.arange(L)[:, None] == b[None, :]).astype(np.float32)


def dot(a, b, dims, precision=None):
    return lax.dot_general(a, b, (dims, ((), ())), precision=precision, preferred_element_type=F32)


NN, NT, TN = ((1,), (0,)), ((1,), (1,)), ((0,), (0,))


def halves(tile):
    low = lax.broadcasted_iota(jnp.int32, tile.shape, 1) < 64
    zero = jnp.zeros_like(tile)
    return jnp.concatenate([jnp.where(low, tile, zero), jnp.where(low, zero, tile)], axis=0)


def offset_sums(square):
    acc = square[:8]
    for k in range(8, L, 8):
        acc = acc + pltpu.roll(square[k : k + 8], L - k, 1)
    row = lax.broadcasted_iota(jnp.int32, acc.shape, 0)
    for bit in (1, 2, 4):
        acc = jnp.where((row & bit) != 0, pltpu.roll(acc, L - bit, 1), acc)
    return jnp.sum(acc, axis=0, keepdims=True)


def cost(us, mib):
    return pl.CostEstimate(flops=int(us * 1e9), bytes_accessed=int(mib * MIB), transcendentals=0)


def place():
    return lax.axis_index("z"), lax.axis_index("x"), lax.axis_index("c")


def pre_kernel(table_ref, gain_ref, pos_ref, picks_ref, ne_ref, r_ref, bvec_ref):
    width = table_ref.shape[1]
    part = width // NX
    wide = table_ref[...].astype(F32)
    r = lax.rsqrt(jnp.sum(wide * wide, axis=1, keepdims=True) * (1.0 / width) + 1e-06)
    r_ref[...] = jnp.broadcast_to(r, r_ref.shape)
    cols = pl.ds(pl.multiple_of(lax.axis_index("x") * part, L), part)
    own = table_ref[:, cols]
    ne_ref[:, :part] = (own.astype(F32) * r * gain_ref[:, cols]).astype(BF16)
    ne_ref[:, part:] = own

    @pl.when(pl.program_id(0) == 0)
    def _():
        bvec_ref[...] = dot(pos_ref[...], picks_ref[...], TN, lax.Precision.HIGHEST) * LOG2E


def prepare(table, gain, pos, picks):
    vocab, width = table.shape
    part = width // NX
    rows = 128
    heads = pos.shape[1]
    return pl.pallas_call(
        pre_kernel,
        grid=(vocab // rows,),
        in_specs=[
            pl.BlockSpec((rows, width), lambda i: (i, 0)),
            pl.BlockSpec((1, width), lambda i: (0, 0)),
            pl.BlockSpec(pos.shape, lambda i: (0, 0)),
            pl.BlockSpec(picks.shape, lambda i: (0, 0)),
        ],
        out_specs=[
            pl.BlockSpec((rows, 2 * part), lambda i: (i, 0)),
            pl.BlockSpec((rows, L), lambda i: (i, 0)),
            pl.BlockSpec((heads, L), lambda i: (0, 0)),
        ],
        out_shape=[
            jax.ShapeDtypeStruct((vocab, 2 * part), BF16),
            jax.ShapeDtypeStruct((vocab, L), F32),
            jax.ShapeDtypeStruct((heads, L), F32),
        ],
        compiler_params=pltpu.CompilerParams(vmem_limit_bytes=12 * MIB),
        cost_estimate=cost(5, 7),
        name="prepare",
    )(table, gain, pos, picks)


def onehot_t(ids_row, vocab):
    v = lax.broadcasted_iota(jnp.int32, (vocab, ids_row.shape[1]), 0)
    return jnp.where(v == ids_row, 1.0, 0.0).astype(BF16)


def packed(notes_ref, slot, what):
    z, x, c = place()
    chip = z * NX + lax.rem(x + NX - slot, NX)
    order = notes_ref[pl.ds(chip * 2 + c, 1), 2, :]
    values = notes_ref[:, what, :]
    found = lax.broadcasted_iota(jnp.int32, values.shape, 0) == order
    return jnp.sum(jnp.where(found, values, 0), axis=0, keepdims=True)


def fwd_kernel(notes_ref, ne_hbm, bvec_hbm, *rest):
    a_refs, (n_ref, p_ref), (e_ref, m_ref, ne_ref, bvec_ref, sems) = rest[:NX], rest[NX : NX + 2], rest[NX + 2 :]
    eighth = ne_ref.shape[0] // 8
    copies = [
        pltpu.make_async_copy(ne_hbm.at[pl.ds(k * eighth, eighth)], ne_ref.at[pl.ds(k * eighth, eighth)], sems.at[k])
        for k in range(8)
    ]
    copies.append(pltpu.make_async_copy(bvec_hbm, bvec_ref, sems.at[8]))
    for copy in copies:
        copy.start()
    vocab, part = ne_ref.shape[0], ne_ref.shape[1] // 2
    pairs = part // L
    first = lax.axis_index("x") * (2 * pairs)
    for s in range(NX):
        seg = jnp.broadcast_to(packed(notes_ref, s, 1), (L, L)).astype(F32)
        m_ref[s] = jnp.where(seg == seg.T, 0.0, -1e30)
    picked = [onehot_t(packed(notes_ref, s, 0), vocab) for s in range(NX)]
    for copy in copies:
        copy.wait()
    for s in range(NX):
        both = dot(picked[s], ne_ref[...], TN)
        n_ref[s] = both[:, :part].astype(BF16)
        e_ref[s] = both[:, part:].astype(BF16)

    @pl.loop(0, pairs, unroll=UF)
    def _(p):
        cols = pl.ds(pl.multiple_of(p * L, L), L)
        biases = [
            pltpu.roll(
                jnp.broadcast_to(bvec_ref[pl.ds(first + 2 * p + k, 1), :], (L, L)),
                0,
                1,
                stride=1,
                stride_axis=0,
            )
            for k in range(2)
        ]
        for s in range(NX):
            tile = n_ref[s, :, cols]
            two = halves(tile)
            mask = m_ref[s]
            raw = dot(two, tile, NT)
            both_p = []
            for k in range(2):
                scores = raw[k * L : (k + 1) * L] * (LOG2E / 64.0) + (biases[k] + mask)
                expo = jnp.exp2(scores - jnp.max(scores, axis=0, keepdims=True))
                probs = expo * (1.0 / jnp.sum(expo, axis=0, keepdims=True))
                both_p.append(probs.astype(BF16))
                p_ref[p, s, k * L : (k + 1) * L] = both_p[-1]
            mixed = dot(jnp.concatenate(both_p, axis=0), two, TN)
            a_refs[s][:, cols] = (e_ref[s, :, cols].astype(F32) + mixed).astype(BF16)


def forward(notes, ne, bvec):
    part = ne.shape[1] // 2
    pairs = part // L
    vmem, hbm = pl.BlockSpec(memory_space=pltpu.VMEM), pl.BlockSpec(memory_space=pltpu.HBM)
    return pl.pallas_call(
        fwd_kernel,
        in_specs=[vmem, hbm, hbm],
        out_specs=[vmem] * (NX + 2),
        out_shape=[jax.ShapeDtypeStruct((L, part), BF16)] * NX
        + [
            jax.ShapeDtypeStruct((NX, L, part), BF16),
            jax.ShapeDtypeStruct((pairs, NX, 2 * L, L), BF16),
        ],
        scratch_shapes=[
            pltpu.VMEM((NX, L, part), BF16),
            pltpu.VMEM((NX, L, L), F32),
            pltpu.VMEM(ne.shape, BF16),
            pltpu.VMEM(bvec.shape, F32),
            pltpu.SemaphoreType.DMA((9,)),
        ],
        compiler_params=pltpu.CompilerParams(vmem_limit_bytes=18 * MIB),
        cost_estimate=cost(8, 7),
        name="forward",
    )(notes, ne, bvec)


def bwd_kernel(notes_ref, ne_ref, r_ref, gain_ref, picks_ref, n_ref, p_ref, *rest):
    g_refs, (mine_ref, other_ref), rest = rest[:NX], rest[NX : NX + 2], rest[NX + 2 :]
    d_ref, rg_ref, o_ref, diag_ref = rest
    vocab, part = ne_ref.shape[0], ne_ref.shape[1] // 2
    pairs = part // L
    blocks = vocab // 16
    _, x, core = place()

    @pl.loop(0, pairs, unroll=UB)
    def _(p):
        cols = pl.ds(pl.multiple_of(p * L, L), L)
        total = [jnp.zeros((L, L), F32)] * 2
        for s in range(NX):
            tile, up = n_ref[s, :, cols], g_refs[s][:, cols]
            rg_ref[pl.ds(s * L, L), cols] = up
            two, ups = halves(tile), halves(up)
            d_all = dot(two, up, NT)
            small = []
            for k in range(2):
                wide = p_ref[p, s, k * L : (k + 1) * L].astype(F32)
                d_probs = d_all[k * L : (k + 1) * L].astype(BF16).astype(F32)
                d_scores = wide * (d_probs - jnp.sum(wide * d_probs, axis=0, keepdims=True))
                total[k] = total[k] + d_scores
                small.append(d_scores.astype(BF16))
            part64 = two * BF16(1.0 / 64.0)
            left = jnp.concatenate([p_ref[p, s, :L], p_ref[p, s, L:]] + small, axis=1)
            d_norm = dot(left, jnp.concatenate([ups, part64], axis=0), NN)
            d_norm = d_norm + dot(jnp.concatenate(small, axis=0), part64, TN)
            d_ref[pl.ds(s * L, L), cols] = d_norm.astype(BF16)
        for k in range(2):
            diag_ref[pl.ds(2 * p + k, 1), :] = offset_sums(total[k])

    for s in range(NX):
        o_ref[:, s * L : (s + 1) * L] = onehot_t(packed(notes_ref, s, 0), vocab)

    def put(tile, value):
        value = value.reshape(blocks, 2, 8, L)
        first, second = value[:, 0], value[:, 1]
        mine_ref[tile] = jnp.where(core == 0, first, second)
        other_ref[tile] = jnp.where(core == 0, second, first)

    r = r_ref[...]
    along = jnp.zeros((vocab, L), F32)
    for f in range(pairs):
        cols = slice(f * L, (f + 1) * L)
        d_act = dot(o_ref[...], rg_ref[:, cols], NN)
        d_norm = dot(o_ref[...], d_ref[:, cols], NN)
        gain = gain_ref[:, pl.ds(pl.multiple_of(x * part + f * L, L), L)]
        own = ne_ref[:, part + f * L : part + (f + 1) * L].astype(F32)
        scaled = d_norm * r
        put(f, d_act + scaled * gain)
        along = along + own * (d_norm * gain)
        g_row = jnp.sum(own * scaled, axis=0, keepdims=True)
        for ref in (mine_ref, other_ref):
            ref[pairs + 1, 0, pl.ds(f, 1), :] = g_row
    put(pairs, along)
    sums = dot(diag_ref[...], picks_ref[...], NT, lax.Precision.HIGHEST)
    for ref in (mine_ref, other_ref):
        ref[pairs + 1, 1] = sums[:8]
        ref[pairs + 1, 2] = sums[8:]
        ref[pairs + 1, 3:] = jnp.zeros((blocks - 3, 8, L), F32)


def backward(notes, ne, r, gain, picks, n, probs, grads):
    vocab, part = ne.shape[0], ne.shape[1] // 2
    pairs = part // L
    vmem = pl.BlockSpec(memory_space=pltpu.VMEM)
    stacked = (pairs + 2, vocab // 16, 8, L)
    out = jax.ShapeDtypeStruct(stacked, F32)
    return pl.pallas_call(
        bwd_kernel,
        in_specs=[vmem] * (7 + NX),
        out_specs=[vmem, vmem],
        out_shape=[out, out],
        scratch_shapes=[
            pltpu.VMEM((NX * L, part), BF16),
            pltpu.VMEM((NX * L, part), BF16),
            pltpu.VMEM((vocab, NX * L), BF16),
            pltpu.VMEM((2 * pairs, L), F32),
        ],
        compiler_params=pltpu.CompilerParams(vmem_limit_bytes=24 * MIB),
        cost_estimate=cost(10, 10),
        name="backward",
    )(notes, ne, r, gain, picks, n, probs, *grads)


def join_kernel(mine_ref, came_ref, out_ref):
    tiles, blocks = mine_ref.shape[0] - 2, mine_ref.shape[1]
    for t in range(tiles):
        out_ref[:, t] = (mine_ref[t] + came_ref[t]).astype(BF16)
    sums = [mine_ref[tiles + 1, t] + came_ref[tiles + 1, t] for t in range(3)]
    out_ref[:, tiles] = jnp.broadcast_to(sums[0].astype(BF16)[None], (blocks, 8, L))
    bias = sums[1] + pltpu.roll(sums[2], 32, 1)
    lane = lax.broadcasted_iota(jnp.int32, (8, L), 1)
    for d in range(blocks):
        along = jnp.sum(mine_ref[tiles, d] + came_ref[tiles, d], axis=1, keepdims=True)
        value = jnp.where(lane == 16, along, bias)
        high = value.astype(BF16).astype(F32)
        out_ref[d, tiles + 1] = (high + pltpu.roll(value - high, 64, 1)).astype(BF16)


def join(mine, came):
    tiles, blocks = mine.shape[:2]
    vmem = pl.BlockSpec(memory_space=pltpu.VMEM)
    return pl.pallas_call(
        join_kernel,
        in_specs=[vmem, vmem],
        out_specs=vmem,
        out_shape=jax.ShapeDtypeStruct((blocks, tiles, 8, L), BF16),
        compiler_params=pltpu.CompilerParams(vmem_limit_bytes=8 * MIB),
        cost_estimate=cost(2, 4),
        name="join",
    )(mine, came)


def last_kernel(parts_ref, table_ref, r_ref, t_ref, g_ref, b_ref, h_ref):
    sources, feats = parts_ref.shape[0], parts_ref.shape[1] - 2
    width = table_ref.shape[1]
    z, x_own, c = place()
    lane = lax.broadcasted_iota(jnp.int32, (8, L), 1)

    def total(x, tile):
        value = parts_ref[x, tile].astype(F32)
        for k in range(1, sources // NX):
            value = value + parts_ref[k * NX + x, tile].astype(F32)
        return value

    along = jnp.zeros((8, 1), F32)
    for x in range(NX):
        value = total(x, feats + 1)
        value = value + pltpu.roll(value, 64, 1)
        along = along + jnp.sum(jnp.where(lane == 16, value, 0.0), axis=1, keepdims=True)
        value = jnp.where(lane == 16, 0.0, value)
        h_ref[x * 16 : x * 16 + 8, :] = value
        h_ref[x * 16 + 8 : x * 16 + 16, :] = pltpu.roll(value, L - 32, 1)
    b_ref[0] = h_ref[...].T[:32]
    at = pl.multiple_of(((z * NX + x_own) * 2 + c) * 8, 8)
    r = r_ref[pl.ds(at, 8), :][:, :1]
    factor = along * (r * r * r) * (1.0 / width)
    for x in range(NX):
        gains = total(x, feats)
        for f in range(feats):
            k = (x * feats + f) * L
            t_ref[0, :, k : k + L] = total(x, f) - table_ref[:, k : k + L].astype(F32) * factor
            g_ref[0:1, k : k + L] = gains[f : f + 1]


def finish(parts, table, r):
    width = table.shape[1]
    vmem = pl.BlockSpec(memory_space=pltpu.VMEM)
    return pl.pallas_call(
        last_kernel,
        in_specs=[vmem, vmem, vmem],
        out_specs=[vmem] * 3,
        out_shape=[
            jax.ShapeDtypeStruct((1, 8, width), F32),
            jax.ShapeDtypeStruct((1, width), F32),
            jax.ShapeDtypeStruct((1, 32, 64), F32),
        ],
        scratch_shapes=[pltpu.VMEM((64, L), F32)],
        compiler_params=pltpu.CompilerParams(vmem_limit_bytes=8 * MIB),
        cost_estimate=cost(2, 2),
        name="finish",
    )(parts, table, r)


def local(picks, token_ids, segment_ids, row_order, embed_table, norm_gain, position_bias, returned_grad):
    x, z, c = lax.axis_index("x"), lax.axis_index("z"), lax.axis_index("c")
    table, gain, pos, grad = embed_table[0], norm_gain, position_bias[0], returned_grad[0]
    part = table.shape[1] // NX
    sections = lax.axis_size("section")

    def send(value, steps, along):
        pairs = [
            (i * sections + j, (i + steps) % NX * sections + (j + along) % sections)
            for i in range(NX)
            for j in range(sections)
        ]
        return lax.ppermute(value, ("x", "section"), pairs)

    grads = [
        send(lax.dynamic_slice(grad, (0, lax.rem(x + s, NX) * part), (L, part)), s, -1) for s in range(NX)
    ]

    table_then, grads[2] = lax.optimization_barrier((table, grads[2]))
    ne, r, bvec = prepare(table_then, gain, pos, picks[:32])
    count = 64
    note = [jnp.broadcast_to(v.reshape(1, 1, -1), (count, 1, L)) for v in (token_ids, segment_ids, row_order)]
    notes = lax.all_to_all(jnp.concatenate(note, axis=1), ("z", "x", "c"), 0, 0)

    *acts, normed, probs = forward(notes, ne, bvec)
    pieces = {s: send(acts[s], -s, 1) for s in (2, 1, 3, 0)}
    mine, other = backward(notes, ne, r, gain, picks, normed, probs, grads)
    came = lax.ppermute(other, "c", [(0, 1), (1, 0)])
    handed = jnp.zeros((L, NX * part), BF16)
    for s in (2, 1, 3, 0):
        handed = lax.dynamic_update_slice(handed, pieces[s], (0, lax.rem(x + s, NX) * part))

    parts = lax.all_to_all(join(mine, came), ("z", "x"), 0, 0)
    rows = lax.dynamic_slice(table, (((z * NX + x) * 2 + c) * 8, 0), (8, table.shape[1]))
    return (handed[None],) + tuple(finish(parts, rows, r))


def solution(mesh):
    fine = Mesh(mesh.devices.reshape(8, NX, 2, 4), ("z", "x", "c", "section"))
    dp = ("z", "x", "c")
    placed = (
        P(),
        P("section", dp, None),
        P("section", dp, None),
        P("section", dp),
        P("section", None, None),
        P("section", None),
        P("section", None, None),
        P("section", dp, None),
    )
    mapped = jax.shard_map(
        local,
        mesh=fine,
        in_specs=placed,
        out_specs=(
            P("section", dp, None),
            P("section", dp, None),
            P("section", None),
            P("section", None, None),
        ),
        check_vma=False,
    )
    return lambda *args: mapped(jnp.asarray(bucket_picks()), *args)
```

```python
import functools

import jax
import jax.numpy as jnp
import numpy as np
from jax import lax
from jax.experimental import pallas as pl
from jax.experimental.pallas import tpu as pltpu
from jax.sharding import Mesh, PartitionSpec as P

F32, BF16 = jnp.float32, jnp.bfloat16
LIMITS = (12, 16, 23, 32, 45, 64, 91)
UF, UB = 8, 8
LOG2E = 1.4426950408889634
L = 128
NX = 4
MIB = 1024 * 1024
SPARE = 24


def bucket_picks():
    c = np.arange(L)
    r = -np.where(c < 64, c, c - L)
    a = np.abs(r)
    b = np.minimum(a, 8) + sum((a >= t).astype(np.int64) for t in LIMITS) + 16 * (r > 0)
    return (np.arange(L)[:, None] == b[None, :]).astype(np.float32)


def dot(a, b, dims, precision=None):
    return lax.dot_general(a, b, (dims, ((), ())), precision=precision, preferred_element_type=F32)


NN, NT, TN = ((1,), (0,)), ((1,), (1,)), ((0,), (0,))


def halves(tile):
    low = lax.broadcasted_iota(jnp.int32, tile.shape, 1) < 64
    zero = jnp.zeros_like(tile)
    return jnp.concatenate([jnp.where(low, tile, zero), jnp.where(low, zero, tile)], axis=0)


def offset_sums(square):
    acc = square[:8]
    for k in range(8, L, 8):
        acc = acc + pltpu.roll(square[k : k + 8], L - k, 1)
    row = lax.broadcasted_iota(jnp.int32, acc.shape, 0)
    for bit in (1, 2, 4):
        acc = jnp.where((row & bit) != 0, pltpu.roll(acc, L - bit, 1), acc)
    return jnp.sum(acc, axis=0, keepdims=True)


def cost(us, mib):
    return pl.CostEstimate(flops=int(us * 1e9), bytes_accessed=int(mib * MIB), transcendentals=0)


def place():
    return lax.axis_index("z"), lax.axis_index("x"), lax.axis_index("c")


def pre_kernel(table_ref, gain_ref, pos_ref, picks_ref, ne_ref, r_ref, bvec_ref):
    width = table_ref.shape[1]
    part = width // NX
    wide = table_ref[...].astype(F32)
    r = lax.rsqrt(jnp.sum(wide * wide, axis=1, keepdims=True) * (1.0 / width) + 1e-06)
    r_ref[...] = jnp.broadcast_to(r, r_ref.shape)
    cols = pl.ds(pl.multiple_of(lax.axis_index("x") * part, L), part)
    own = table_ref[:, cols]
    ne_ref[:, :part] = (own.astype(F32) * r * gain_ref[:, cols]).astype(BF16)
    ne_ref[:, part:] = own

    @pl.when(pl.program_id(0) == 0)
    def _():
        bvec_ref[...] = dot(pos_ref[...], picks_ref[...], TN, lax.Precision.HIGHEST) * LOG2E


def prepare(table, gain, pos, picks):
    vocab, width = table.shape
    part = width // NX
    rows = 128
    heads = pos.shape[1]
    return pl.pallas_call(
        pre_kernel,
        grid=(vocab // rows,),
        in_specs=[
            pl.BlockSpec((rows, width), lambda i: (i, 0)),
            pl.BlockSpec((1, width), lambda i: (0, 0)),
            pl.BlockSpec(pos.shape, lambda i: (0, 0)),
            pl.BlockSpec(picks.shape, lambda i: (0, 0)),
        ],
        out_specs=[
            pl.BlockSpec((rows, 2 * part), lambda i: (i, 0)),
            pl.BlockSpec((rows, L), lambda i: (i, 0)),
            pl.BlockSpec((heads, L), lambda i: (0, 0)),
        ],
        out_shape=[
            jax.ShapeDtypeStruct((vocab * SPARE, 2 * part), BF16),
            jax.ShapeDtypeStruct((vocab, L), F32),
            jax.ShapeDtypeStruct((heads, L), F32),
        ],
        compiler_params=pltpu.CompilerParams(vmem_limit_bytes=12 * MIB),
        cost_estimate=cost(5, 7),
        name="prepare",
    )(table, gain, pos, picks)


def onehot_t(ids_row, vocab):
    v = lax.broadcasted_iota(jnp.int32, (vocab, ids_row.shape[1]), 0)
    return jnp.where(v == ids_row, 1.0, 0.0).astype(BF16)


def packed(notes_ref, slot, what):
    z, x, c = place()
    chip = z * NX + lax.rem(x + NX - slot, NX)
    order = notes_ref[pl.ds(chip * 2 + c, 1), 2, :]
    values = notes_ref[:, what, :]
    found = lax.broadcasted_iota(jnp.int32, values.shape, 0) == order
    return jnp.sum(jnp.where(found, values, 0), axis=0, keepdims=True)


def fwd_kernel(notes_ref, ne_hbm, bvec_hbm, *rest):
    a_refs, (n_ref, p_ref), (e_ref, m_ref, ne_ref, bvec_ref, sems) = rest[:NX], rest[NX : NX + 2], rest[NX + 2 :]
    eighth = ne_ref.shape[0] // 8
    copies = [
        pltpu.make_async_copy(ne_hbm.at[pl.ds(k * eighth, eighth)], ne_ref.at[pl.ds(k * eighth, eighth)], sems.at[k])
        for k in range(8)
    ]
    copies.append(pltpu.make_async_copy(bvec_hbm, bvec_ref, sems.at[8]))
    for copy in copies:
        copy.start()
    vocab, part = ne_ref.shape[0], ne_ref.shape[1] // 2
    pairs = part // L
    first = lax.axis_index("x") * (2 * pairs)
    for s in range(NX):
        seg = jnp.broadcast_to(packed(notes_ref, s, 1), (L, L)).astype(F32)
        m_ref[s] = jnp.where(seg == seg.T, 0.0, -1e30)
    picked = [onehot_t(packed(notes_ref, s, 0), vocab) for s in range(NX)]
    for copy in copies:
        copy.wait()
    for s in range(NX):
        both = dot(picked[s], ne_ref[...], TN)
        n_ref[s] = both[:, :part].astype(BF16)
        e_ref[s] = both[:, part:].astype(BF16)

    @pl.loop(0, pairs, unroll=UF)
    def _(p):
        cols = pl.ds(pl.multiple_of(p * L, L), L)
        biases = [
            pltpu.roll(
                jnp.broadcast_to(bvec_ref[pl.ds(first + 2 * p + k, 1), :], (L, L)),
                0,
                1,
                stride=1,
                stride_axis=0,
            )
            for k in range(2)
        ]
        for s in range(NX):
            tile = n_ref[s, :, cols]
            two = halves(tile)
            mask = m_ref[s]
            raw = dot(two, tile, NT)
            both_p = []
            for k in range(2):
                scores = raw[k * L : (k + 1) * L] * (LOG2E / 64.0) + (biases[k] + mask)
                expo = jnp.exp2(scores - jnp.max(scores, axis=0, keepdims=True))
                probs = expo * (1.0 / jnp.sum(expo, axis=0, keepdims=True))
                both_p.append(probs.astype(BF16))
                p_ref[p, s, k * L : (k + 1) * L] = both_p[-1]
            mixed = dot(jnp.concatenate(both_p, axis=0), two, TN)
            a_refs[s][:, cols] = (e_ref[s, :, cols].astype(F32) + mixed).astype(BF16)


def forward(notes, ne, bvec, vocab):
    part = ne.shape[1] // 2
    pairs = part // L
    vmem, hbm = pl.BlockSpec(memory_space=pltpu.VMEM), pl.BlockSpec(memory_space=pltpu.HBM)
    return pl.pallas_call(
        fwd_kernel,
        in_specs=[vmem, hbm, hbm],
        out_specs=[vmem] * (NX + 2),
        out_shape=[jax.ShapeDtypeStruct((L, part), BF16)] * NX
        + [
            jax.ShapeDtypeStruct((NX, L, part), BF16),
            jax.ShapeDtypeStruct((pairs, NX, 2 * L, L), BF16),
        ],
        scratch_shapes=[
            pltpu.VMEM((NX, L, part), BF16),
            pltpu.VMEM((NX, L, L), F32),
            pltpu.VMEM((vocab, 2 * part), BF16),
            pltpu.VMEM(bvec.shape, F32),
            pltpu.SemaphoreType.DMA((9,)),
        ],
        compiler_params=pltpu.CompilerParams(vmem_limit_bytes=18 * MIB),
        cost_estimate=cost(8, 7),
        name="forward",
    )(notes, ne, bvec)


def bwd_kernel(notes_ref, ne_hbm, r_ref, gain_ref, picks_ref, n_ref, p_ref, *rest):
    g_refs, (mine_hbm, other_ref), rest = rest[:NX], rest[NX : NX + 2], rest[NX + 2 :]
    d_ref, rg_ref, o_ref, diag_ref, own_ref, mine_ref, own_sem, sems = rest
    vocab, part = own_ref.shape
    fetch = pltpu.make_async_copy(ne_hbm.at[pl.ds(0, vocab), pl.ds(part, part)], own_ref, own_sem)
    fetch.start()
    pairs = part // L
    blocks = vocab // 16
    _, x, core = place()

    @pl.loop(0, pairs, unroll=UB)
    def _(p):
        cols = pl.ds(pl.multiple_of(p * L, L), L)
        total = [jnp.zeros((L, L), F32)] * 2
        for s in range(NX):
            tile, up = n_ref[s, :, cols], g_refs[s][:, cols]
            rg_ref[pl.ds(s * L, L), cols] = up
            two, ups = halves(tile), halves(up)
            d_all = dot(two, up, NT)
            small = []
            for k in range(2):
                wide = p_ref[p, s, k * L : (k + 1) * L].astype(F32)
                d_probs = d_all[k * L : (k + 1) * L].astype(BF16).astype(F32)
                d_scores = wide * (d_probs - jnp.sum(wide * d_probs, axis=0, keepdims=True))
                total[k] = total[k] + d_scores
                small.append(d_scores.astype(BF16))
            part64 = two * BF16(1.0 / 64.0)
            left = jnp.concatenate([p_ref[p, s, :L], p_ref[p, s, L:]] + small, axis=1)
            d_norm = dot(left, jnp.concatenate([ups, part64], axis=0), NN)
            d_norm = d_norm + dot(jnp.concatenate(small, axis=0), part64, TN)
            d_ref[pl.ds(s * L, L), cols] = d_norm.astype(BF16)
        for k in range(2):
            diag_ref[pl.ds(2 * p + k, 1), :] = offset_sums(total[k])

    for s in range(NX):
        o_ref[:, s * L : (s + 1) * L] = onehot_t(packed(notes_ref, s, 0), vocab)

    fetch.wait()
    copies = []

    def out(tile):
        copies.append(pltpu.make_async_copy(mine_ref.at[tile], mine_hbm.at[tile], sems.at[tile]))
        copies[-1].start()

    def put(tile, value):
        value = value.reshape(blocks, 2, 8, L)
        first, second = value[:, 0], value[:, 1]
        mine_ref[tile] = jnp.where(core == 0, first, second)
        other_ref[tile] = jnp.where(core == 0, second, first)
        out(tile)

    r = r_ref[...]
    along = jnp.zeros((vocab, L), F32)
    for f in range(pairs):
        cols = slice(f * L, (f + 1) * L)
        d_act = dot(o_ref[...], rg_ref[:, cols], NN)
        d_norm = dot(o_ref[...], d_ref[:, cols], NN)
        gain = gain_ref[:, pl.ds(pl.multiple_of(x * part + f * L, L), L)]
        own = own_ref[:, cols].astype(F32)
        scaled = d_norm * r
        put(f, d_act + scaled * gain)
        along = along + own * (d_norm * gain)
        g_row = jnp.sum(own * scaled, axis=0, keepdims=True)
        for ref in (mine_ref, other_ref):
            ref[pairs + 1, 0, pl.ds(f, 1), :] = g_row
    put(pairs, along)
    sums = dot(diag_ref[...], picks_ref[...], NT, lax.Precision.HIGHEST)
    for ref in (mine_ref, other_ref):
        ref[pairs + 1, 1] = sums[:8]
        ref[pairs + 1, 2] = sums[8:]
        ref[pairs + 1, 3:] = jnp.zeros((blocks - 3, 8, L), F32)
    out(pairs + 1)
    for copy in copies:
        copy.wait()


def backward(notes, ne, r, gain, picks, n, probs, grads):
    vocab, part = r.shape[0], ne.shape[1] // 2
    pairs = part // L
    vmem, hbm = pl.BlockSpec(memory_space=pltpu.VMEM), pl.BlockSpec(memory_space=pltpu.HBM)
    stacked = (pairs + 2, vocab // 16, 8, L)
    spare = (stacked[0] * 32,) + stacked[1:]
    return pl.pallas_call(
        bwd_kernel,
        in_specs=[vmem, hbm] + [vmem] * (5 + NX),
        out_specs=[hbm, vmem],
        out_shape=[jax.ShapeDtypeStruct(spare, F32), jax.ShapeDtypeStruct(stacked, F32)],
        scratch_shapes=[
            pltpu.VMEM((NX * L, part), BF16),
            pltpu.VMEM((NX * L, part), BF16),
            pltpu.VMEM((vocab, NX * L), BF16),
            pltpu.VMEM((2 * pairs, L), F32),
            pltpu.VMEM((vocab, part), BF16),
            pltpu.VMEM(stacked, F32),
            pltpu.SemaphoreType.DMA,
            pltpu.SemaphoreType.DMA((pairs + 2,)),
        ],
        compiler_params=pltpu.CompilerParams(vmem_limit_bytes=24 * MIB),
        cost_estimate=cost(10, 10),
        name="backward",
    )(notes, ne, r, gain, picks, n, probs, *grads)


def join_kernel(mine_hbm, came_ref, out_ref, mine_ref, sems):
    tiles, blocks = mine_ref.shape[0] - 2, mine_ref.shape[1]
    copies = [pltpu.make_async_copy(mine_hbm.at[t], mine_ref.at[t], sems.at[t]) for t in range(tiles + 2)]
    for copy in copies:
        copy.start()
    for t in range(tiles):
        copies[t].wait()
        out_ref[:, t] = (mine_ref[t] + came_ref[t]).astype(BF16)
    copies[tiles].wait()
    copies[tiles + 1].wait()
    sums = [mine_ref[tiles + 1, t] + came_ref[tiles + 1, t] for t in range(3)]
    out_ref[:, tiles] = jnp.broadcast_to(sums[0].astype(BF16)[None], (blocks, 8, L))
    bias = sums[1] + pltpu.roll(sums[2], 32, 1)
    lane = lax.broadcasted_iota(jnp.int32, (8, L), 1)
    for d in range(blocks):
        along = jnp.sum(mine_ref[tiles, d] + came_ref[tiles, d], axis=1, keepdims=True)
        value = jnp.where(lane == 16, along, bias)
        high = value.astype(BF16).astype(F32)
        out_ref[d, tiles + 1] = (high + pltpu.roll(value - high, 64, 1)).astype(BF16)


def join(mine, came):
    tiles, blocks = came.shape[:2]
    vmem, hbm = pl.BlockSpec(memory_space=pltpu.VMEM), pl.BlockSpec(memory_space=pltpu.HBM)
    return pl.pallas_call(
        join_kernel,
        in_specs=[hbm, vmem],
        out_specs=vmem,
        out_shape=jax.ShapeDtypeStruct((blocks, tiles, 8, L), BF16),
        scratch_shapes=[pltpu.VMEM(came.shape, F32), pltpu.SemaphoreType.DMA((tiles,))],
        compiler_params=pltpu.CompilerParams(vmem_limit_bytes=40 * MIB),
        cost_estimate=cost(2, 4),
        name="join",
    )(mine, came)


def last_kernel(parts_ref, table_ref, r_ref, t_ref, g_ref, b_ref, h_ref):
    sources, feats = parts_ref.shape[0], parts_ref.shape[1] - 2
    width = table_ref.shape[1]
    z, x_own, c = place()
    lane = lax.broadcasted_iota(jnp.int32, (8, L), 1)

    def total(x, tile):
        value = parts_ref[x, tile].astype(F32)
        for k in range(1, sources // NX):
            value = value + parts_ref[k * NX + x, tile].astype(F32)
        return value

    along = jnp.zeros((8, 1), F32)
    for x in range(NX):
        value = total(x, feats + 1)
        value = value + pltpu.roll(value, 64, 1)
        along = along + jnp.sum(jnp.where(lane == 16, value, 0.0), axis=1, keepdims=True)
        value = jnp.where(lane == 16, 0.0, value)
        h_ref[x * 16 : x * 16 + 8, :] = value
        h_ref[x * 16 + 8 : x * 16 + 16, :] = pltpu.roll(value, L - 32, 1)
    b_ref[0] = h_ref[...].T[:32]
    at = pl.multiple_of(((z * NX + x_own) * 2 + c) * 8, 8)
    r = r_ref[pl.ds(at, 8), :][:, :1]
    factor = along * (r * r * r) * (1.0 / width)
    for x in range(NX):
        gains = total(x, feats)
        for f in range(feats):
            k = (x * feats + f) * L
            t_ref[0, :, k : k + L] = total(x, f) - table_ref[:, k : k + L].astype(F32) * factor
            g_ref[0:1, k : k + L] = gains[f : f + 1]


def finish(parts, table, r):
    width = table.shape[1]
    vmem = pl.BlockSpec(memory_space=pltpu.VMEM)
    return pl.pallas_call(
        last_kernel,
        in_specs=[vmem, vmem, vmem],
        out_specs=[vmem] * 3,
        out_shape=[
            jax.ShapeDtypeStruct((1, 8, width), F32),
            jax.ShapeDtypeStruct((1, width), F32),
            jax.ShapeDtypeStruct((1, 32, 64), F32),
        ],
        scratch_shapes=[pltpu.VMEM((64, L), F32)],
        compiler_params=pltpu.CompilerParams(vmem_limit_bytes=8 * MIB),
        cost_estimate=cost(2, 2),
        name="finish",
    )(parts, table, r)


def local(picks, token_ids, segment_ids, row_order, embed_table, norm_gain, position_bias, returned_grad):
    x, z, c = lax.axis_index("x"), lax.axis_index("z"), lax.axis_index("c")
    table, gain, pos, grad = embed_table[0], norm_gain, position_bias[0], returned_grad[0]
    part = table.shape[1] // NX
    sections = lax.axis_size("section")

    def send(value, steps, along):
        pairs = [
            (i * sections + j, (i + steps) % NX * sections + (j + along) % sections)
            for i in range(NX)
            for j in range(sections)
        ]
        return lax.ppermute(value, ("x", "section"), pairs)

    grads = [
        send(lax.dynamic_slice(grad, (0, lax.rem(x + s, NX) * part), (L, part)), s, -1) for s in range(NX)
    ]

    table_then, grads[1], grads[2] = lax.optimization_barrier((table, grads[1], grads[2]))
    ne, r, bvec = prepare(table_then, gain, pos, picks[:32])
    count = 64
    note = [jnp.broadcast_to(v.reshape(1, 1, -1), (count, 1, L)) for v in (token_ids, segment_ids, row_order)]
    notes = lax.all_to_all(jnp.concatenate(note, axis=1), ("z", "x", "c"), 0, 0)

    *acts, normed, probs = forward(notes, ne, bvec, table.shape[0])
    pieces = {s: send(acts[s], -s, 1) for s in (2, 1, 3, 0)}
    mine, other = backward(notes, ne, r, gain, picks, normed, probs, grads)
    came = lax.ppermute(other, "c", [(0, 1), (1, 0)])
    handed = jnp.zeros((L, NX * part), BF16)
    for s in (2, 1, 3, 0):
        handed = lax.dynamic_update_slice(handed, pieces[s], (0, lax.rem(x + s, NX) * part))

    parts = lax.all_to_all(join(mine, came), ("z", "x"), 0, 0)
    rows = lax.dynamic_slice(table, (((z * NX + x) * 2 + c) * 8, 0), (8, table.shape[1]))
    return (handed[None],) + tuple(finish(parts, rows, r))


def solution(mesh):
    fine = Mesh(mesh.devices.reshape(8, NX, 2, 4), ("z", "x", "c", "section"))
    dp = ("z", "x", "c")
    placed = (
        P(),
        P("section", dp, None),
        P("section", dp, None),
        P("section", dp),
        P("section", None, None),
        P("section", None),
        P("section", None, None),
        P("section", dp, None),
    )
    mapped = jax.shard_map(
        local,
        mesh=fine,
        in_specs=placed,
        out_specs=(
            P("section", dp, None),
            P("section", dp, None),
            P("section", None),
            P("section", None, None),
        ),
        check_vma=False,
    )
    return lambda *args: mapped(jnp.asarray(bucket_picks()), *args)
```

```python
import functools

import jax
import jax.numpy as jnp
import numpy as np
from jax import lax
from jax.experimental import pallas as pl
from jax.experimental.pallas import tpu as pltpu
from jax.sharding import Mesh, PartitionSpec as P

F32, BF16 = jnp.float32, jnp.bfloat16
LIMITS = (12, 16, 23, 32, 45, 64, 91)
UF, UB = 8, 8
LOG2E = 1.4426950408889634
L = 128
NX = 4
MIB = 1024 * 1024


def bucket_picks():
    c = np.arange(L)
    r = -np.where(c < 64, c, c - L)
    a = np.abs(r)
    b = np.minimum(a, 8) + sum((a >= t).astype(np.int64) for t in LIMITS) + 16 * (r > 0)
    return (np.arange(L)[:, None] == b[None, :]).astype(np.float32)


def dot(a, b, dims, precision=None):
    return lax.dot_general(a, b, (dims, ((), ())), precision=precision, preferred_element_type=F32)


NN, NT, TN = ((1,), (0,)), ((1,), (1,)), ((0,), (0,))


def halves(tile):
    low = lax.broadcasted_iota(jnp.int32, tile.shape, 1) < 64
    zero = jnp.zeros_like(tile)
    return jnp.concatenate([jnp.where(low, tile, zero), jnp.where(low, zero, tile)], axis=0)


def offset_sums(square):
    acc = square[:8]
    for k in range(8, L, 8):
        acc = acc + pltpu.roll(square[k : k + 8], L - k, 1)
    row = lax.broadcasted_iota(jnp.int32, acc.shape, 0)
    for bit in (1, 2, 4):
        acc = jnp.where((row & bit) != 0, pltpu.roll(acc, L - bit, 1), acc)
    return jnp.sum(acc, axis=0, keepdims=True)


def cost(us, mib):
    return pl.CostEstimate(flops=int(us * 1e9), bytes_accessed=int(mib * MIB), transcendentals=0)


def place():
    return lax.axis_index("z"), lax.axis_index("x"), lax.axis_index("c")


def pre_kernel(table_ref, gain_ref, pos_ref, picks_ref, ne_ref, r_ref, bvec_ref):
    width = table_ref.shape[1]
    part = width // NX
    wide = table_ref[...].astype(F32)
    r = lax.rsqrt(jnp.sum(wide * wide, axis=1, keepdims=True) * (1.0 / width) + 1e-06)
    r_ref[...] = jnp.broadcast_to(r, r_ref.shape)
    cols = pl.ds(pl.multiple_of(lax.axis_index("x") * part, L), part)
    own = table_ref[:, cols]
    ne_ref[:, :part] = (own.astype(F32) * r * gain_ref[:, cols]).astype(BF16)
    ne_ref[:, part:] = own

    @pl.when(pl.program_id(0) == 0)
    def _():
        bvec_ref[...] = dot(pos_ref[...], picks_ref[...], TN, lax.Precision.HIGHEST) * LOG2E


def prepare(table, gain, pos, picks):
    vocab, width = table.shape
    part = width // NX
    rows = 128
    heads = pos.shape[1]
    return pl.pallas_call(
        pre_kernel,
        grid=(vocab // rows,),
        in_specs=[
            pl.BlockSpec((rows, width), lambda i: (i, 0)),
            pl.BlockSpec((1, width), lambda i: (0, 0)),
            pl.BlockSpec(pos.shape, lambda i: (0, 0)),
            pl.BlockSpec(picks.shape, lambda i: (0, 0)),
        ],
        out_specs=[
            pl.BlockSpec((rows, 2 * part), lambda i: (i, 0)),
            pl.BlockSpec((rows, L), lambda i: (i, 0)),
            pl.BlockSpec((heads, L), lambda i: (0, 0)),
        ],
        out_shape=[
            jax.ShapeDtypeStruct((vocab, 2 * part), BF16),
            jax.ShapeDtypeStruct((vocab, L), F32),
            jax.ShapeDtypeStruct((heads, L), F32),
        ],
        compiler_params=pltpu.CompilerParams(vmem_limit_bytes=12 * MIB),
        cost_estimate=cost(5, 7),
        name="prepare",
    )(table, gain, pos, picks)


def onehot_t(ids_row, vocab):
    v = lax.broadcasted_iota(jnp.int32, (vocab, ids_row.shape[1]), 0)
    return jnp.where(v == ids_row, 1.0, 0.0).astype(BF16)


def packed(notes_ref, slot, what):
    z, x, c = place()
    chip = z * NX + lax.rem(x + NX - slot, NX)
    order = notes_ref[pl.ds(chip * 2 + c, 1), 2, :]
    values = notes_ref[:, what, :]
    found = lax.broadcasted_iota(jnp.int32, values.shape, 0) == order
    return jnp.sum(jnp.where(found, values, 0), axis=0, keepdims=True)


def fwd_kernel(notes_ref, ne_hbm, bvec_hbm, *rest):
    a_refs, (n_ref, p_ref), (e_ref, m_ref, ne_ref, bvec_ref, sems) = rest[:NX], rest[NX : NX + 2], rest[NX + 2 :]
    eighth = ne_ref.shape[0] // 8
    copies = [
        pltpu.make_async_copy(ne_hbm.at[pl.ds(k * eighth, eighth)], ne_ref.at[pl.ds(k * eighth, eighth)], sems.at[k])
        for k in range(8)
    ]
    copies.append(pltpu.make_async_copy(bvec_hbm, bvec_ref, sems.at[8]))
    for copy in copies:
        copy.start()
    vocab, part = ne_ref.shape[0], ne_ref.shape[1] // 2
    pairs = part // L
    first = lax.axis_index("x") * (2 * pairs)
    for s in range(NX):
        seg = jnp.broadcast_to(packed(notes_ref, s, 1), (L, L)).astype(F32)
        m_ref[s] = jnp.where(seg == seg.T, 0.0, -1e30)
    picked = [onehot_t(packed(notes_ref, s, 0), vocab) for s in range(NX)]
    for copy in copies:
        copy.wait()
    for s in range(NX):
        both = dot(picked[s], ne_ref[...], TN)
        n_ref[s] = both[:, :part].astype(BF16)
        e_ref[s] = both[:, part:].astype(BF16)

    @pl.loop(0, pairs, unroll=UF)
    def _(p):
        cols = pl.ds(pl.multiple_of(p * L, L), L)
        biases = [
            pltpu.roll(
                jnp.broadcast_to(bvec_ref[pl.ds(first + 2 * p + k, 1), :], (L, L)),
                0,
                1,
                stride=1,
                stride_axis=0,
            )
            for k in range(2)
        ]
        for s in range(NX):
            tile = n_ref[s, :, cols]
            two = halves(tile)
            mask = m_ref[s]
            raw = dot(two, tile, NT)
            both_p = []
            for k in range(2):
                scores = raw[k * L : (k + 1) * L] * (LOG2E / 64.0) + (biases[k] + mask)
                expo = jnp.exp2(scores - jnp.max(scores, axis=0, keepdims=True))
                probs = expo * (1.0 / jnp.sum(expo, axis=0, keepdims=True))
                both_p.append(probs.astype(BF16))
                p_ref[p, s, k * L : (k + 1) * L] = both_p[-1]
            mixed = dot(jnp.concatenate(both_p, axis=0), two, TN)
            a_refs[s][:, cols] = (e_ref[s, :, cols].astype(F32) + mixed).astype(BF16)


def forward(notes, ne, bvec):
    part = ne.shape[1] // 2
    pairs = part // L
    vmem, hbm = pl.BlockSpec(memory_space=pltpu.VMEM), pl.BlockSpec(memory_space=pltpu.HBM)
    return pl.pallas_call(
        fwd_kernel,
        in_specs=[vmem, hbm, hbm],
        out_specs=[vmem] * (NX + 2),
        out_shape=[jax.ShapeDtypeStruct((L, part), BF16)] * NX
        + [
            jax.ShapeDtypeStruct((NX, L, part), BF16),
            jax.ShapeDtypeStruct((pairs, NX, 2 * L, L), BF16),
        ],
        scratch_shapes=[
            pltpu.VMEM((NX, L, part), BF16),
            pltpu.VMEM((NX, L, L), F32),
            pltpu.VMEM(ne.shape, BF16),
            pltpu.VMEM(bvec.shape, F32),
            pltpu.SemaphoreType.DMA((9,)),
        ],
        compiler_params=pltpu.CompilerParams(vmem_limit_bytes=18 * MIB),
        cost_estimate=cost(8, 7),
        name="forward",
    )(notes, ne, bvec)


def bwd_kernel(notes_ref, ne_ref, r_ref, gain_ref, picks_ref, n_ref, p_ref, *rest):
    g_refs, (mine_ref, other_ref), rest = rest[:NX], rest[NX : NX + 2], rest[NX + 2 :]
    d_ref, rg_ref, o_ref, diag_ref = rest
    vocab, part = ne_ref.shape[0], ne_ref.shape[1] // 2
    pairs = part // L
    blocks = vocab // 16
    _, x, core = place()

    @pl.loop(0, pairs, unroll=UB)
    def _(p):
        cols = pl.ds(pl.multiple_of(p * L, L), L)
        total = [jnp.zeros((L, L), F32)] * 2
        for s in range(NX):
            tile, up = n_ref[s, :, cols], g_refs[s][:, cols]
            rg_ref[pl.ds(s * L, L), cols] = up
            two, ups = halves(tile), halves(up)
            d_all = dot(two, up, NT)
            small = []
            for k in range(2):
                wide = p_ref[p, s, k * L : (k + 1) * L].astype(F32)
                d_probs = d_all[k * L : (k + 1) * L].astype(BF16).astype(F32)
                d_scores = wide * (d_probs - jnp.sum(wide * d_probs, axis=0, keepdims=True))
                total[k] = total[k] + d_scores
                small.append(d_scores.astype(BF16))
            part64 = two * BF16(1.0 / 64.0)
            left = jnp.concatenate([p_ref[p, s, :L], p_ref[p, s, L:]] + small, axis=1)
            d_norm = dot(left, jnp.concatenate([ups, part64], axis=0), NN)
            d_norm = d_norm + dot(jnp.concatenate(small, axis=0), part64, TN)
            d_ref[pl.ds(s * L, L), cols] = d_norm.astype(BF16)
        for k in range(2):
            diag_ref[pl.ds(2 * p + k, 1), :] = offset_sums(total[k])

    for s in range(NX):
        o_ref[:, s * L : (s + 1) * L] = onehot_t(packed(notes_ref, s, 0), vocab)

    def put(tile, value):
        value = value.reshape(blocks, 2, 8, L)
        first, second = value[:, 0], value[:, 1]
        mine_ref[tile] = jnp.where(core == 0, first, second)
        other_ref[tile] = jnp.where(core == 0, second, first)

    r = r_ref[...]
    along = jnp.zeros((vocab, L), F32)
    for f in range(pairs):
        cols = slice(f * L, (f + 1) * L)
        d_act = dot(o_ref[...], rg_ref[:, cols], NN)
        d_norm = dot(o_ref[...], d_ref[:, cols], NN)
        gain = gain_ref[:, pl.ds(pl.multiple_of(x * part + f * L, L), L)]
        own = ne_ref[:, part + f * L : part + (f + 1) * L].astype(F32)
        scaled = d_norm * r
        put(f, d_act + scaled * gain)
        along = along + own * (d_norm * gain)
        g_row = jnp.sum(own * scaled, axis=0, keepdims=True)
        for ref in (mine_ref, other_ref):
            ref[pairs + 1, 0, pl.ds(f, 1), :] = g_row
    put(pairs, along)
    sums = dot(diag_ref[...], picks_ref[...], NT, lax.Precision.HIGHEST)
    for ref in (mine_ref, other_ref):
        ref[pairs + 1, 1] = sums[:8]
        ref[pairs + 1, 2] = sums[8:]
        ref[pairs + 1, 3:] = jnp.zeros((blocks - 3, 8, L), F32)


def backward(notes, ne, r, gain, picks, n, probs, grads):
    vocab, part = ne.shape[0], ne.shape[1] // 2
    pairs = part // L
    vmem = pl.BlockSpec(memory_space=pltpu.VMEM)
    stacked = (pairs + 2, vocab // 16, 8, L)
    out = jax.ShapeDtypeStruct(stacked, F32)
    return pl.pallas_call(
        bwd_kernel,
        in_specs=[vmem] * (7 + NX),
        out_specs=[vmem, vmem],
        out_shape=[out, out],
        scratch_shapes=[
            pltpu.VMEM((NX * L, part), BF16),
            pltpu.VMEM((NX * L, part), BF16),
            pltpu.VMEM((vocab, NX * L), BF16),
            pltpu.VMEM((2 * pairs, L), F32),
        ],
        compiler_params=pltpu.CompilerParams(vmem_limit_bytes=24 * MIB),
        cost_estimate=cost(10, 10),
        name="backward",
    )(notes, ne, r, gain, picks, n, probs, *grads)


def join_kernel(mine_ref, came_ref, out_ref):
    tiles, blocks = mine_ref.shape[0] - 2, mine_ref.shape[1]
    for t in range(tiles):
        out_ref[:, t] = (mine_ref[t] + came_ref[t]).astype(BF16)
    sums = [mine_ref[tiles + 1, t] + came_ref[tiles + 1, t] for t in range(3)]
    out_ref[:, tiles] = jnp.broadcast_to(sums[0].astype(BF16)[None], (blocks, 8, L))
    bias = sums[1] + pltpu.roll(sums[2], 32, 1)
    lane = lax.broadcasted_iota(jnp.int32, (8, L), 1)
    for d in range(blocks):
        along = jnp.sum(mine_ref[tiles, d] + came_ref[tiles, d], axis=1, keepdims=True)
        value = jnp.where(lane == 16, along, bias)
        high = value.astype(BF16).astype(F32)
        out_ref[d, tiles + 1] = (high + pltpu.roll(value - high, 64, 1)).astype(BF16)


def join(mine, came):
    tiles, blocks = mine.shape[:2]
    vmem = pl.BlockSpec(memory_space=pltpu.VMEM)
    return pl.pallas_call(
        join_kernel,
        in_specs=[vmem, vmem],
        out_specs=vmem,
        out_shape=jax.ShapeDtypeStruct((blocks, tiles, 8, L), BF16),
        compiler_params=pltpu.CompilerParams(vmem_limit_bytes=8 * MIB),
        cost_estimate=cost(2, 4),
        name="join",
    )(mine, came)


def last_kernel(parts_ref, table_ref, r_ref, t_ref, g_ref, b_ref, h_ref):
    sources, feats = parts_ref.shape[0], parts_ref.shape[1] - 2
    width = table_ref.shape[1]
    z, x_own, c = place()
    lane = lax.broadcasted_iota(jnp.int32, (8, L), 1)

    def total(x, tile):
        value = parts_ref[x, tile].astype(F32)
        for k in range(1, sources // NX):
            value = value + parts_ref[k * NX + x, tile].astype(F32)
        return value

    along = jnp.zeros((8, 1), F32)
    for x in range(NX):
        value = total(x, feats + 1)
        value = value + pltpu.roll(value, 64, 1)
        along = along + jnp.sum(jnp.where(lane == 16, value, 0.0), axis=1, keepdims=True)
        value = jnp.where(lane == 16, 0.0, value)
        h_ref[x * 16 : x * 16 + 8, :] = value
        h_ref[x * 16 + 8 : x * 16 + 16, :] = pltpu.roll(value, L - 32, 1)
    b_ref[0] = h_ref[...].T[:32]
    at = pl.multiple_of(((z * NX + x_own) * 2 + c) * 8, 8)
    r = r_ref[pl.ds(at, 8), :][:, :1]
    factor = along * (r * r * r) * (1.0 / width)
    for x in range(NX):
        gains = total(x, feats)
        for f in range(feats):
            k = (x * feats + f) * L
            t_ref[0, :, k : k + L] = total(x, f) - table_ref[:, k : k + L].astype(F32) * factor
            g_ref[0:1, k : k + L] = gains[f : f + 1]


def finish(parts, table, r):
    width = table.shape[1]
    vmem = pl.BlockSpec(memory_space=pltpu.VMEM)
    return pl.pallas_call(
        last_kernel,
        in_specs=[vmem, vmem, vmem],
        out_specs=[vmem] * 3,
        out_shape=[
            jax.ShapeDtypeStruct((1, 8, width), F32),
            jax.ShapeDtypeStruct((1, width), F32),
            jax.ShapeDtypeStruct((1, 32, 64), F32),
        ],
        scratch_shapes=[pltpu.VMEM((64, L), F32)],
        compiler_params=pltpu.CompilerParams(vmem_limit_bytes=8 * MIB),
        cost_estimate=cost(2, 2),
        name="finish",
    )(parts, table, r)


def local(picks, token_ids, segment_ids, row_order, embed_table, norm_gain, position_bias, returned_grad):
    x, z, c = lax.axis_index("x"), lax.axis_index("z"), lax.axis_index("c")
    table, gain, pos, grad = embed_table[0], norm_gain, position_bias[0], returned_grad[0]
    part = table.shape[1] // NX
    sections = lax.axis_size("section")

    def send(value, steps, along):
        pairs = [
            (i * sections + j, (i + steps) % NX * sections + (j + along) % sections)
            for i in range(NX)
            for j in range(sections)
        ]
        return lax.ppermute(value, ("x", "section"), pairs)

    grads = [
        send(lax.dynamic_slice(grad, (0, lax.rem(x + s, NX) * part), (L, part)), s, -1) for s in range(NX)
    ]

    table_then, grads[0], grads[1] = lax.optimization_barrier((table, grads[0], grads[1]))
    ne, r, bvec = prepare(table_then, gain, pos, picks[:32])
    count = 64
    note = [jnp.broadcast_to(v.reshape(1, 1, -1), (count, 1, L)) for v in (token_ids, segment_ids, row_order)]
    notes = lax.all_to_all(jnp.concatenate(note, axis=1), ("z", "x", "c"), 0, 0)

    *acts, normed, probs = forward(notes, ne, bvec)
    pieces = {s: send(acts[s], -s, 1) for s in (2, 1, 3, 0)}
    mine, other = backward(notes, ne, r, gain, picks, normed, probs, grads)
    came = lax.ppermute(other, "c", [(0, 1), (1, 0)])
    handed = jnp.zeros((L, NX * part), BF16)
    for s in (2, 1, 3, 0):
        handed = lax.dynamic_update_slice(handed, pieces[s], (0, lax.rem(x + s, NX) * part))

    parts = lax.all_to_all(join(mine, came), ("z", "x"), 0, 0)
    rows = lax.dynamic_slice(table, (((z * NX + x) * 2 + c) * 8, 0), (8, table.shape[1]))
    return (handed[None],) + tuple(finish(parts, rows, r))


def solution(mesh):
    fine = Mesh(mesh.devices.reshape(8, NX, 2, 4), ("z", "x", "c", "section"))
    dp = ("z", "x", "c")
    placed = (
        P(),
        P("section", dp, None),
        P("section", dp, None),
        P("section", dp),
        P("section", None, None),
        P("section", None),
        P("section", None, None),
        P("section", dp, None),
    )
    mapped = jax.shard_map(
        local,
        mesh=fine,
        in_specs=placed,
        out_specs=(
            P("section", dp, None),
            P("section", dp, None),
            P("section", None),
            P("section", None, None),
        ),
        check_vma=False,
    )
    return lambda *args: mapped(jnp.asarray(bucket_picks()), *args)
```

```python
import functools

import jax
import jax.numpy as jnp
import numpy as np
from jax import lax
from jax.experimental import pallas as pl
from jax.experimental.pallas import tpu as pltpu
from jax.sharding import Mesh, PartitionSpec as P

F32, BF16 = jnp.float32, jnp.bfloat16
LIMITS = (12, 16, 23, 32, 45, 64, 91)
UF, UB = 8, 8
LOG2E = 1.4426950408889634
L = 128
NX = 4
MIB = 1024 * 1024


def bucket_picks():
    c = np.arange(L)
    r = -np.where(c < 64, c, c - L)
    a = np.abs(r)
    b = np.minimum(a, 8) + sum((a >= t).astype(np.int64) for t in LIMITS) + 16 * (r > 0)
    return (np.arange(L)[:, None] == b[None, :]).astype(np.float32)


def dot(a, b, dims, precision=None):
    return lax.dot_general(a, b, (dims, ((), ())), precision=precision, preferred_element_type=F32)


NN, NT, TN = ((1,), (0,)), ((1,), (1,)), ((0,), (0,))


def halves(tile):
    low = lax.broadcasted_iota(jnp.int32, tile.shape, 1) < 64
    zero = jnp.zeros_like(tile)
    return jnp.concatenate([jnp.where(low, tile, zero), jnp.where(low, zero, tile)], axis=0)


def offset_sums(square):
    acc = square[:8]
    for k in range(8, L, 8):
        acc = acc + pltpu.roll(square[k : k + 8], L - k, 1)
    row = lax.broadcasted_iota(jnp.int32, acc.shape, 0)
    for bit in (1, 2, 4):
        acc = jnp.where((row & bit) != 0, pltpu.roll(acc, L - bit, 1), acc)
    return jnp.sum(acc, axis=0, keepdims=True)


def cost(us, mib):
    return pl.CostEstimate(flops=int(us * 1e9), bytes_accessed=int(mib * MIB), transcendentals=0)


def place():
    return lax.axis_index("z"), lax.axis_index("x"), lax.axis_index("c")


def pre_kernel(table_ref, gain_ref, pos_ref, picks_ref, ne_ref, r_ref, bvec_ref):
    width = table_ref.shape[1]
    part = width // NX
    wide = table_ref[...].astype(F32)
    r = lax.rsqrt(jnp.sum(wide * wide, axis=1, keepdims=True) * (1.0 / width) + 1e-06)
    r_ref[...] = jnp.broadcast_to(r, r_ref.shape)
    cols = pl.ds(pl.multiple_of(lax.axis_index("x") * part, L), part)
    own = table_ref[:, cols]
    ne_ref[:, :part] = (own.astype(F32) * r * gain_ref[:, cols]).astype(BF16)
    ne_ref[:, part:] = own

    @pl.when(pl.program_id(0) == 0)
    def _():
        bvec_ref[...] = dot(pos_ref[...], picks_ref[...], TN, lax.Precision.HIGHEST) * LOG2E


def prepare(table, gain, pos, picks):
    vocab, width = table.shape
    part = width // NX
    rows = 128
    heads = pos.shape[1]
    return pl.pallas_call(
        pre_kernel,
        grid=(vocab // rows,),
        in_specs=[
            pl.BlockSpec((rows, width), lambda i: (i, 0)),
            pl.BlockSpec((1, width), lambda i: (0, 0)),
            pl.BlockSpec(pos.shape, lambda i: (0, 0)),
            pl.BlockSpec(picks.shape, lambda i: (0, 0)),
        ],
        out_specs=[
            pl.BlockSpec((rows, 2 * part), lambda i: (i, 0)),
            pl.BlockSpec((rows, L), lambda i: (i, 0)),
            pl.BlockSpec((heads, L), lambda i: (0, 0)),
        ],
        out_shape=[
            jax.ShapeDtypeStruct((vocab, 2 * part), BF16),
            jax.ShapeDtypeStruct((vocab, L), F32),
            jax.ShapeDtypeStruct((heads, L), F32),
        ],
        compiler_params=pltpu.CompilerParams(vmem_limit_bytes=12 * MIB),
        cost_estimate=cost(5, 7),
        name="prepare",
    )(table, gain, pos, picks)


def onehot_t(ids_row, vocab):
    v = lax.broadcasted_iota(jnp.int32, (vocab, ids_row.shape[1]), 0)
    return jnp.where(v == ids_row, 1.0, 0.0).astype(BF16)


def packed(notes_ref, slot, what):
    z, x, c = place()
    chip = z * NX + lax.rem(x + NX - slot, NX)
    order = notes_ref[pl.ds(chip * 2 + c, 1), 2, :]
    values = notes_ref[:, what, :]
    found = lax.broadcasted_iota(jnp.int32, values.shape, 0) == order
    return jnp.sum(jnp.where(found, values, 0), axis=0, keepdims=True)


def fwd_kernel(notes_ref, ne_hbm, bvec_hbm, *rest):
    a_refs, (n_ref, p_ref), (e_ref, m_ref, ne_ref, bvec_ref, sems) = rest[:NX], rest[NX : NX + 2], rest[NX + 2 :]
    eighth = ne_ref.shape[0] // 8
    copies = [
        pltpu.make_async_copy(ne_hbm.at[pl.ds(k * eighth, eighth)], ne_ref.at[pl.ds(k * eighth, eighth)], sems.at[k])
        for k in range(8)
    ]
    copies.append(pltpu.make_async_copy(bvec_hbm, bvec_ref, sems.at[8]))
    for copy in copies:
        copy.start()
    vocab, part = ne_ref.shape[0], ne_ref.shape[1] // 2
    pairs = part // L
    first = lax.axis_index("x") * (2 * pairs)
    for s in range(NX):
        seg = jnp.broadcast_to(packed(notes_ref, s, 1), (L, L)).astype(F32)
        m_ref[s] = jnp.where(seg == seg.T, 0.0, -1e30)
    picked = [onehot_t(packed(notes_ref, s, 0), vocab) for s in range(NX)]
    for copy in copies:
        copy.wait()
    for s in range(NX):
        both = dot(picked[s], ne_ref[...], TN)
        n_ref[s] = both[:, :part].astype(BF16)
        e_ref[s] = both[:, part:].astype(BF16)

    @pl.loop(0, pairs, unroll=UF)
    def _(p):
        cols = pl.ds(pl.multiple_of(p * L, L), L)
        biases = [
            pltpu.roll(
                jnp.broadcast_to(bvec_ref[pl.ds(first + 2 * p + k, 1), :], (L, L)),
                0,
                1,
                stride=1,
                stride_axis=0,
            )
            for k in range(2)
        ]
        for s in range(NX):
            tile = n_ref[s, :, cols]
            two = halves(tile)
            mask = m_ref[s]
            raw = dot(two, tile, NT)
            both_p = []
            for k in range(2):
                scores = raw[k * L : (k + 1) * L] * (LOG2E / 64.0) + (biases[k] + mask)
                expo = jnp.exp2(scores - jnp.max(scores, axis=0, keepdims=True))
                probs = expo * (1.0 / jnp.sum(expo, axis=0, keepdims=True))
                both_p.append(probs.astype(BF16))
                p_ref[p, s, k * L : (k + 1) * L] = both_p[-1]
            mixed = dot(jnp.concatenate(both_p, axis=0), two, TN)
            a_refs[s][:, cols] = (e_ref[s, :, cols].astype(F32) + mixed).astype(BF16)


def forward(notes, ne, bvec):
    part = ne.shape[1] // 2
    pairs = part // L
    vmem, hbm = pl.BlockSpec(memory_space=pltpu.VMEM), pl.BlockSpec(memory_space=pltpu.HBM)
    return pl.pallas_call(
        fwd_kernel,
        in_specs=[vmem, hbm, hbm],
        out_specs=[vmem] * (NX + 2),
        out_shape=[jax.ShapeDtypeStruct((L, part), BF16)] * NX
        + [
            jax.ShapeDtypeStruct((NX, L, part), BF16),
            jax.ShapeDtypeStruct((pairs, NX, 2 * L, L), BF16),
        ],
        scratch_shapes=[
            pltpu.VMEM((NX, L, part), BF16),
            pltpu.VMEM((NX, L, L), F32),
            pltpu.VMEM(ne.shape, BF16),
            pltpu.VMEM(bvec.shape, F32),
            pltpu.SemaphoreType.DMA((9,)),
        ],
        compiler_params=pltpu.CompilerParams(vmem_limit_bytes=18 * MIB),
        cost_estimate=cost(8, 7),
        name="forward",
    )(notes, ne, bvec)


def bwd_kernel(notes_ref, ne_ref, r_ref, gain_ref, picks_ref, n_ref, p_ref, *rest):
    g_refs, (mine_ref, other_ref), rest = rest[:NX], rest[NX : NX + 2], rest[NX + 2 :]
    d_ref, rg_ref, o_ref, diag_ref = rest
    vocab, part = ne_ref.shape[0], ne_ref.shape[1] // 2
    pairs = part // L
    blocks = vocab // 16
    _, x, core = place()

    @pl.loop(0, pairs, unroll=UB)
    def _(p):
        cols = pl.ds(pl.multiple_of(p * L, L), L)
        total = [jnp.zeros((L, L), F32)] * 2
        for s in range(NX):
            tile, up = n_ref[s, :, cols], g_refs[s][:, cols]
            rg_ref[pl.ds(s * L, L), cols] = up
            two, ups = halves(tile), halves(up)
            d_all = dot(two, up, NT)
            small = []
            for k in range(2):
                wide = p_ref[p, s, k * L : (k + 1) * L].astype(F32)
                d_probs = d_all[k * L : (k + 1) * L].astype(BF16).astype(F32)
                d_scores = wide * (d_probs - jnp.sum(wide * d_probs, axis=0, keepdims=True))
                total[k] = total[k] + d_scores
                small.append(d_scores.astype(BF16))
            part64 = two * BF16(1.0 / 64.0)
            left = jnp.concatenate([p_ref[p, s, :L], p_ref[p, s, L:]] + small, axis=1)
            d_norm = dot(left, jnp.concatenate([ups, part64], axis=0), NN)
            d_norm = d_norm + dot(jnp.concatenate(small, axis=0), part64, TN)
            d_ref[pl.ds(s * L, L), cols] = d_norm.astype(BF16)
        for k in range(2):
            diag_ref[pl.ds(2 * p + k, 1), :] = offset_sums(total[k])

    for s in range(NX):
        o_ref[:, s * L : (s + 1) * L] = onehot_t(packed(notes_ref, s, 0), vocab)

    def put(tile, value):
        value = value.reshape(blocks, 2, 8, L)
        first, second = value[:, 0], value[:, 1]
        mine_ref[tile] = jnp.where(core == 0, first, second)
        other_ref[tile] = jnp.where(core == 0, second, first)

    r = r_ref[...]
    along = jnp.zeros((vocab, L), F32)
    for f in range(pairs):
        cols = slice(f * L, (f + 1) * L)
        d_act = dot(o_ref[...], rg_ref[:, cols], NN)
        d_norm = dot(o_ref[...], d_ref[:, cols], NN)
        gain = gain_ref[:, pl.ds(pl.multiple_of(x * part + f * L, L), L)]
        own = ne_ref[:, part + f * L : part + (f + 1) * L].astype(F32)
        scaled = d_norm * r
        put(f, d_act + scaled * gain)
        along = along + own * (d_norm * gain)
        g_row = jnp.sum(own * scaled, axis=0, keepdims=True)
        for ref in (mine_ref, other_ref):
            ref[pairs + 1, 0, pl.ds(f, 1), :] = g_row
    put(pairs, along)
    sums = dot(diag_ref[...], picks_ref[...], NT, lax.Precision.HIGHEST)
    for ref in (mine_ref, other_ref):
        ref[pairs + 1, 1] = sums[:8]
        ref[pairs + 1, 2] = sums[8:]
        ref[pairs + 1, 3:] = jnp.zeros((blocks - 3, 8, L), F32)


def backward(notes, ne, r, gain, picks, n, probs, grads):
    vocab, part = ne.shape[0], ne.shape[1] // 2
    pairs = part // L
    vmem = pl.BlockSpec(memory_space=pltpu.VMEM)
    stacked = (pairs + 2, vocab // 16, 8, L)
    out = jax.ShapeDtypeStruct(stacked, F32)
    return pl.pallas_call(
        bwd_kernel,
        in_specs=[vmem] * (7 + NX),
        out_specs=[vmem, vmem],
        out_shape=[out, out],
        scratch_shapes=[
            pltpu.VMEM((NX * L, part), BF16),
            pltpu.VMEM((NX * L, part), BF16),
            pltpu.VMEM((vocab, NX * L), BF16),
            pltpu.VMEM((2 * pairs, L), F32),
        ],
        compiler_params=pltpu.CompilerParams(vmem_limit_bytes=24 * MIB),
        cost_estimate=cost(10, 10),
        name="backward",
    )(notes, ne, r, gain, picks, n, probs, *grads)


def join_kernel(mine_ref, came_ref, out_ref):
    tiles, blocks = mine_ref.shape[0] - 2, mine_ref.shape[1]
    for t in range(tiles):
        out_ref[:, t] = (mine_ref[t] + came_ref[t]).astype(BF16)
    sums = [mine_ref[tiles + 1, t] + came_ref[tiles + 1, t] for t in range(3)]
    out_ref[:, tiles] = jnp.broadcast_to(sums[0].astype(BF16)[None], (blocks, 8, L))
    bias = sums[1] + pltpu.roll(sums[2], 32, 1)
    lane = lax.broadcasted_iota(jnp.int32, (8, L), 1)
    for d in range(blocks):
        along = jnp.sum(mine_ref[tiles, d] + came_ref[tiles, d], axis=1, keepdims=True)
        value = jnp.where(lane == 16, along, bias)
        high = value.astype(BF16).astype(F32)
        out_ref[d, tiles + 1] = (high + pltpu.roll(value - high, 64, 1)).astype(BF16)


def join(mine, came):
    tiles, blocks = mine.shape[:2]
    vmem = pl.BlockSpec(memory_space=pltpu.VMEM)
    return pl.pallas_call(
        join_kernel,
        in_specs=[vmem, vmem],
        out_specs=vmem,
        out_shape=jax.ShapeDtypeStruct((blocks, tiles, 8, L), BF16),
        compiler_params=pltpu.CompilerParams(vmem_limit_bytes=8 * MIB),
        cost_estimate=cost(2, 4),
        name="join",
    )(mine, came)


def last_kernel(parts_ref, table_ref, r_ref, t_ref, g_ref, b_ref, h_ref):
    sources, feats = parts_ref.shape[0], parts_ref.shape[1] - 2
    width = table_ref.shape[1]
    z, x_own, c = place()
    lane = lax.broadcasted_iota(jnp.int32, (8, L), 1)

    def total(x, tile):
        value = parts_ref[x, tile].astype(F32)
        for k in range(1, sources // NX):
            value = value + parts_ref[k * NX + x, tile].astype(F32)
        return value

    along = jnp.zeros((8, 1), F32)
    for x in range(NX):
        value = total(x, feats + 1)
        value = value + pltpu.roll(value, 64, 1)
        along = along + jnp.sum(jnp.where(lane == 16, value, 0.0), axis=1, keepdims=True)
        value = jnp.where(lane == 16, 0.0, value)
        h_ref[x * 16 : x * 16 + 8, :] = value
        h_ref[x * 16 + 8 : x * 16 + 16, :] = pltpu.roll(value, L - 32, 1)
    b_ref[0] = h_ref[...].T[:32]
    at = pl.multiple_of(((z * NX + x_own) * 2 + c) * 8, 8)
    r = r_ref[pl.ds(at, 8), :][:, :1]
    factor = along * (r * r * r) * (1.0 / width)
    for x in range(NX):
        gains = total(x, feats)
        for f in range(feats):
            k = (x * feats + f) * L
            t_ref[0, :, k : k + L] = total(x, f) - table_ref[:, k : k + L].astype(F32) * factor
            g_ref[0:1, k : k + L] = gains[f : f + 1]


def finish(parts, table, r):
    width = table.shape[1]
    vmem = pl.BlockSpec(memory_space=pltpu.VMEM)
    return pl.pallas_call(
        last_kernel,
        in_specs=[vmem, vmem, vmem],
        out_specs=[vmem] * 3,
        out_shape=[
            jax.ShapeDtypeStruct((1, 8, width), F32),
            jax.ShapeDtypeStruct((1, width), F32),
            jax.ShapeDtypeStruct((1, 32, 64), F32),
        ],
        scratch_shapes=[pltpu.VMEM((64, L), F32)],
        compiler_params=pltpu.CompilerParams(vmem_limit_bytes=8 * MIB),
        cost_estimate=cost(2, 2),
        name="finish",
    )(parts, table, r)


def local(picks, token_ids, segment_ids, row_order, embed_table, norm_gain, position_bias, returned_grad):
    x, z, c = lax.axis_index("x"), lax.axis_index("z"), lax.axis_index("c")
    table, gain, pos, grad = embed_table[0], norm_gain, position_bias[0], returned_grad[0]
    part = table.shape[1] // NX
    sections = lax.axis_size("section")

    def send(value, steps, along):
        pairs = [
            (i * sections + j, (i + steps) % NX * sections + (j + along) % sections)
            for i in range(NX)
            for j in range(sections)
        ]
        return lax.ppermute(value, ("x", "section"), pairs)

    grads = [
        send(lax.dynamic_slice(grad, (0, lax.rem(x + s, NX) * part), (L, part)), s, -1) for s in range(NX)
    ]

    table_then, grads[0], grads[1] = lax.optimization_barrier((table, grads[0], grads[1]))
    ne, r, bvec = prepare(table_then, gain, pos, picks[:32])
    count = 64
    kind = lax.broadcasted_iota(jnp.int32, (count, 3, L), 1)
    note = jnp.where(kind == 0, token_ids, jnp.where(kind == 1, segment_ids, row_order[:, :, None]))
    notes = lax.all_to_all(note, ("z", "x", "c"), 0, 0)

    *acts, normed, probs = forward(notes, ne, bvec)
    pieces = {s: send(acts[s], -s, 1) for s in (2, 1, 3, 0)}
    mine, other = backward(notes, ne, r, gain, picks, normed, probs, grads)
    came = lax.ppermute(other, "c", [(0, 1), (1, 0)])
    handed = jnp.zeros((L, NX * part), BF16)
    for s in (2, 1, 3, 0):
        handed = lax.dynamic_update_slice(handed, pieces[s], (0, lax.rem(x + s, NX) * part))

    parts = lax.all_to_all(join(mine, came), ("z", "x"), 0, 0)
    rows = lax.dynamic_slice(table, (((z * NX + x) * 2 + c) * 8, 0), (8, table.shape[1]))
    return (handed[None],) + tuple(finish(parts, rows, r))


def solution(mesh):
    fine = Mesh(mesh.devices.reshape(8, NX, 2, 4), ("z", "x", "c", "section"))
    dp = ("z", "x", "c")
    placed = (
        P(),
        P("section", dp, None),
        P("section", dp, None),
        P("section", dp),
        P("section", None, None),
        P("section", None),
        P("section", None, None),
        P("section", dp, None),
    )
    mapped = jax.shard_map(
        local,
        mesh=fine,
        in_specs=placed,
        out_specs=(
            P("section", dp, None),
            P("section", dp, None),
            P("section", None),
            P("section", None, None),
        ),
        check_vma=False,
    )
    return lambda *args: mapped(jnp.asarray(bucket_picks()), *args)
```

```python
import functools

import jax
import jax.numpy as jnp
import numpy as np
from jax import lax
from jax.experimental import pallas as pl
from jax.experimental.pallas import tpu as pltpu
from jax.sharding import Mesh, PartitionSpec as P

F32, BF16 = jnp.float32, jnp.bfloat16
LIMITS = (12, 16, 23, 32, 45, 64, 91)
UF, UB = 8, 8
LOG2E = 1.4426950408889634
L = 128
NX = 4
MIB = 1024 * 1024


def bucket_picks():
    c = np.arange(L)
    r = -np.where(c < 64, c, c - L)
    a = np.abs(r)
    b = np.minimum(a, 8) + sum((a >= t).astype(np.int64) for t in LIMITS) + 16 * (r > 0)
    return (np.arange(L)[:, None] == b[None, :]).astype(np.float32)


def dot(a, b, dims, precision=None):
    return lax.dot_general(a, b, (dims, ((), ())), precision=precision, preferred_element_type=F32)


NN, NT, TN = ((1,), (0,)), ((1,), (1,)), ((0,), (0,))


def halves(tile):
    low = lax.broadcasted_iota(jnp.int32, tile.shape, 1) < 64
    zero = jnp.zeros_like(tile)
    return jnp.concatenate([jnp.where(low, tile, zero), jnp.where(low, zero, tile)], axis=0)


def offset_sums(square):
    acc = square[:8]
    for k in range(8, L, 8):
        acc = acc + pltpu.roll(square[k : k + 8], L - k, 1)
    row = lax.broadcasted_iota(jnp.int32, acc.shape, 0)
    for bit in (1, 2, 4):
        acc = jnp.where((row & bit) != 0, pltpu.roll(acc, L - bit, 1), acc)
    return jnp.sum(acc, axis=0, keepdims=True)


def cost(us, mib):
    return pl.CostEstimate(flops=int(us * 1e9), bytes_accessed=int(mib * MIB), transcendentals=0)


def place():
    return lax.axis_index("z"), lax.axis_index("x"), lax.axis_index("c")


def pre_kernel(table_ref, gain_ref, pos_ref, picks_ref, ne_ref, r_ref, bvec_ref):
    width = table_ref.shape[1]
    part = width // NX
    wide = table_ref[...].astype(F32)
    r = lax.rsqrt(jnp.sum(wide * wide, axis=1, keepdims=True) * (1.0 / width) + 1e-06)
    r_ref[...] = jnp.broadcast_to(r, r_ref.shape)
    cols = pl.ds(pl.multiple_of(lax.axis_index("x") * part, L), part)
    own = table_ref[:, cols]
    ne_ref[:, :part] = (own.astype(F32) * r * gain_ref[:, cols]).astype(BF16)
    ne_ref[:, part:] = own

    @pl.when(pl.program_id(0) == 0)
    def _():
        bvec_ref[...] = dot(pos_ref[...], picks_ref[...], TN, lax.Precision.HIGHEST) * LOG2E


def prepare(table, gain, pos, picks):
    vocab, width = table.shape
    part = width // NX
    rows = 128
    heads = pos.shape[1]
    return pl.pallas_call(
        pre_kernel,
        grid=(vocab // rows,),
        in_specs=[
            pl.BlockSpec((rows, width), lambda i: (i, 0)),
            pl.BlockSpec((1, width), lambda i: (0, 0)),
            pl.BlockSpec(pos.shape, lambda i: (0, 0)),
            pl.BlockSpec(picks.shape, lambda i: (0, 0)),
        ],
        out_specs=[
            pl.BlockSpec((rows, 2 * part), lambda i: (i, 0)),
            pl.BlockSpec((rows, L), lambda i: (i, 0)),
            pl.BlockSpec((heads, L), lambda i: (0, 0)),
        ],
        out_shape=[
            jax.ShapeDtypeStruct((vocab, 2 * part), BF16),
            jax.ShapeDtypeStruct((vocab, L), F32),
            jax.ShapeDtypeStruct((heads, L), F32),
        ],
        compiler_params=pltpu.CompilerParams(vmem_limit_bytes=12 * MIB),
        cost_estimate=cost(5, 7),
        name="prepare",
    )(table, gain, pos, picks)


def onehot_t(ids_row, vocab):
    v = lax.broadcasted_iota(jnp.int32, (vocab, ids_row.shape[1]), 0)
    return jnp.where(v == ids_row, 1.0, 0.0).astype(BF16)


def packed(notes_ref, slot, what):
    z, x, c = place()
    chip = z * NX + lax.rem(x + NX - slot, NX)
    order = notes_ref[pl.ds(chip * 2 + c, 1), 2, :]
    values = notes_ref[:, what, :]
    found = lax.broadcasted_iota(jnp.int32, values.shape, 0) == order
    return jnp.sum(jnp.where(found, values, 0), axis=0, keepdims=True)


def fwd_kernel(notes_ref, ne_hbm, bvec_hbm, *rest):
    a_refs, (n_ref, p_ref), (e_ref, m_ref, ne_ref, bvec_ref, sems) = rest[:NX], rest[NX : NX + 2], rest[NX + 2 :]
    eighth = ne_ref.shape[0] // 8
    copies = [
        pltpu.make_async_copy(ne_hbm.at[pl.ds(k * eighth, eighth)], ne_ref.at[pl.ds(k * eighth, eighth)], sems.at[k])
        for k in range(8)
    ]
    copies.append(pltpu.make_async_copy(bvec_hbm, bvec_ref, sems.at[8]))
    for copy in copies:
        copy.start()
    vocab, part = ne_ref.shape[0], ne_ref.shape[1] // 2
    pairs = part // L
    first = lax.axis_index("x") * (2 * pairs)
    for s in range(NX):
        seg = jnp.broadcast_to(packed(notes_ref, s, 1), (L, L)).astype(F32)
        m_ref[s] = jnp.where(seg == seg.T, 0.0, -1e30)
    picked = [onehot_t(packed(notes_ref, s, 0), vocab) for s in range(NX)]
    for copy in copies:
        copy.wait()
    for s in range(NX):
        both = dot(picked[s], ne_ref[...], TN)
        n_ref[s] = both[:, :part].astype(BF16)
        e_ref[s] = both[:, part:].astype(BF16)

    @pl.loop(0, pairs, unroll=UF)
    def _(p):
        cols = pl.ds(pl.multiple_of(p * L, L), L)
        biases = [
            pltpu.roll(
                jnp.broadcast_to(bvec_ref[pl.ds(first + 2 * p + k, 1), :], (L, L)),
                0,
                1,
                stride=1,
                stride_axis=0,
            )
            for k in range(2)
        ]
        for s in range(NX):
            tile = n_ref[s, :, cols]
            two = halves(tile)
            mask = m_ref[s]
            raw = dot(two, tile, NT)
            both_p = []
            for k in range(2):
                scores = raw[k * L : (k + 1) * L] * (LOG2E / 64.0) + (biases[k] + mask)
                expo = jnp.exp2(scores - jnp.max(scores, axis=0, keepdims=True))
                probs = expo * (1.0 / jnp.sum(expo, axis=0, keepdims=True))
                both_p.append(probs.astype(BF16))
                p_ref[p, s, k * L : (k + 1) * L] = both_p[-1]
            mixed = dot(jnp.concatenate(both_p, axis=0), two, TN)
            a_refs[s][:, cols] = (e_ref[s, :, cols].astype(F32) + mixed).astype(BF16)


def forward(notes, ne, bvec):
    part = ne.shape[1] // 2
    pairs = part // L
    vmem, hbm = pl.BlockSpec(memory_space=pltpu.VMEM), pl.BlockSpec(memory_space=pltpu.HBM)
    return pl.pallas_call(
        fwd_kernel,
        in_specs=[vmem, hbm, hbm],
        out_specs=[vmem] * (NX + 2),
        out_shape=[jax.ShapeDtypeStruct((L, part), BF16)] * NX
        + [
            jax.ShapeDtypeStruct((NX, L, part), BF16),
            jax.ShapeDtypeStruct((pairs, NX, 2 * L, L), BF16),
        ],
        scratch_shapes=[
            pltpu.VMEM((NX, L, part), BF16),
            pltpu.VMEM((NX, L, L), F32),
            pltpu.VMEM(ne.shape, BF16),
            pltpu.VMEM(bvec.shape, F32),
            pltpu.SemaphoreType.DMA((9,)),
        ],
        compiler_params=pltpu.CompilerParams(vmem_limit_bytes=18 * MIB),
        cost_estimate=cost(8, 7),
        name="forward",
    )(notes, ne, bvec)


def bwd_kernel(notes_ref, ne_ref, r_ref, gain_ref, picks_ref, n_ref, p_ref, *rest):
    g_refs, (mine_ref, other_ref), rest = rest[:NX], rest[NX : NX + 2], rest[NX + 2 :]
    d_ref, rg_ref, o_ref, diag_ref, rows_ref = rest
    vocab, part = ne_ref.shape[0], ne_ref.shape[1] // 2
    pairs = part // L
    blocks = vocab // 16
    _, x, core = place()

    @pl.loop(0, pairs, unroll=UB)
    def _(p):
        cols = pl.ds(pl.multiple_of(p * L, L), L)
        total = [jnp.zeros((L, L), F32)] * 2
        for s in range(NX):
            tile, up = n_ref[s, :, cols], g_refs[s][:, cols]
            rg_ref[pl.ds(s * L, L), cols] = up
            two, ups = halves(tile), halves(up)
            d_all = dot(two, up, NT)
            small = []
            for k in range(2):
                wide = p_ref[p, s, k * L : (k + 1) * L].astype(F32)
                d_probs = d_all[k * L : (k + 1) * L].astype(BF16).astype(F32)
                d_scores = wide * (d_probs - jnp.sum(wide * d_probs, axis=0, keepdims=True))
                total[k] = total[k] + d_scores
                small.append(d_scores.astype(BF16))
            part64 = two * BF16(1.0 / 64.0)
            left = jnp.concatenate([p_ref[p, s, :L], p_ref[p, s, L:]] + small, axis=1)
            d_norm = dot(left, jnp.concatenate([ups, part64], axis=0), NN)
            d_norm = d_norm + dot(jnp.concatenate(small, axis=0), part64, TN)
            d_ref[pl.ds(s * L, L), cols] = d_norm.astype(BF16)
        for k in range(2):
            diag_ref[pl.ds(2 * p + k, 1), :] = offset_sums(total[k])

    for s in range(NX):
        o_ref[:, s * L : (s + 1) * L] = onehot_t(packed(notes_ref, s, 0), vocab)

    def put(tile, value):
        value = value.reshape(blocks, 2, 8, L)
        first, second = value[:, 0], value[:, 1]
        mine_ref[tile] = jnp.where(core == 0, first, second).astype(BF16)
        other_ref[tile] = jnp.where(core == 0, second, first).astype(BF16)

    r = r_ref[...]
    along = jnp.zeros((vocab, L), F32)
    for f in range(pairs):
        cols = slice(f * L, (f + 1) * L)
        d_act = dot(o_ref[...], rg_ref[:, cols], NN)
        d_norm = dot(o_ref[...], d_ref[:, cols], NN)
        gain = gain_ref[:, pl.ds(pl.multiple_of(x * part + f * L, L), L)]
        own = ne_ref[:, part + f * L : part + (f + 1) * L].astype(F32)
        scaled = d_norm * r
        put(f, d_act + scaled * gain)
        along = along + own * (d_norm * gain)
        rows_ref[pl.ds(f, 1), :] = jnp.sum(own * scaled, axis=0, keepdims=True)
    put(pairs, along)
    sums = dot(diag_ref[...], picks_ref[...], NT, lax.Precision.HIGHEST)
    for ref in (mine_ref, other_ref):
        for k, value in enumerate((rows_ref[...], sums[:8], sums[8:])):
            high = value.astype(BF16)
            ref[pairs + 1, k] = high
            ref[pairs + 1, k + 3] = (value - high.astype(F32)).astype(BF16)
        ref[pairs + 1, 6:] = jnp.zeros((blocks - 6, 8, L), BF16)


def backward(notes, ne, r, gain, picks, n, probs, grads):
    vocab, part = ne.shape[0], ne.shape[1] // 2
    pairs = part // L
    vmem = pl.BlockSpec(memory_space=pltpu.VMEM)
    stacked = (pairs + 2, vocab // 16, 8, L)
    out = jax.ShapeDtypeStruct(stacked, BF16)
    return pl.pallas_call(
        bwd_kernel,
        in_specs=[vmem] * (7 + NX),
        out_specs=[vmem, vmem],
        out_shape=[out, out],
        scratch_shapes=[
            pltpu.VMEM((NX * L, part), BF16),
            pltpu.VMEM((NX * L, part), BF16),
            pltpu.VMEM((vocab, NX * L), BF16),
            pltpu.VMEM((2 * pairs, L), F32),
            pltpu.VMEM((8, L), F32),
        ],
        compiler_params=pltpu.CompilerParams(vmem_limit_bytes=24 * MIB),
        cost_estimate=cost(10, 10),
        name="backward",
    )(notes, ne, r, gain, picks, n, probs, *grads)


def join_kernel(mine_ref, came_ref, out_ref):
    tiles, blocks = mine_ref.shape[0] - 2, mine_ref.shape[1]
    for t in range(tiles):
        out_ref[:, t] = (mine_ref[t].astype(F32) + came_ref[t].astype(F32)).astype(BF16)
    both = [mine_ref[tiles + 1, t].astype(F32) + came_ref[tiles + 1, t].astype(F32) for t in range(6)]
    sums = [both[t] + both[t + 3] for t in range(3)]
    out_ref[:, tiles] = jnp.broadcast_to(sums[0].astype(BF16)[None], (blocks, 8, L))
    bias = sums[1] + pltpu.roll(sums[2], 32, 1)
    lane = lax.broadcasted_iota(jnp.int32, (8, L), 1)
    for d in range(blocks):
        along = jnp.sum(mine_ref[tiles, d].astype(F32) + came_ref[tiles, d].astype(F32), axis=1, keepdims=True)
        value = jnp.where(lane == 16, along, bias)
        high = value.astype(BF16).astype(F32)
        out_ref[d, tiles + 1] = (high + pltpu.roll(value - high, 64, 1)).astype(BF16)


def join(mine, came):
    tiles, blocks = mine.shape[:2]
    vmem = pl.BlockSpec(memory_space=pltpu.VMEM)
    return pl.pallas_call(
        join_kernel,
        in_specs=[vmem, vmem],
        out_specs=vmem,
        out_shape=jax.ShapeDtypeStruct((blocks, tiles, 8, L), BF16),
        compiler_params=pltpu.CompilerParams(vmem_limit_bytes=8 * MIB),
        cost_estimate=cost(2, 4),
        name="join",
    )(mine, came)


def last_kernel(parts_ref, table_ref, r_ref, t_ref, g_ref, b_ref, h_ref):
    sources, feats = parts_ref.shape[0], parts_ref.shape[1] - 2
    width = table_ref.shape[1]
    z, x_own, c = place()
    lane = lax.broadcasted_iota(jnp.int32, (8, L), 1)

    def total(x, tile):
        value = parts_ref[x, tile].astype(F32)
        for k in range(1, sources // NX):
            value = value + parts_ref[k * NX + x, tile].astype(F32)
        return value

    along = jnp.zeros((8, 1), F32)
    for x in range(NX):
        value = total(x, feats + 1)
        value = value + pltpu.roll(value, 64, 1)
        along = along + jnp.sum(jnp.where(lane == 16, value, 0.0), axis=1, keepdims=True)
        value = jnp.where(lane == 16, 0.0, value)
        h_ref[x * 16 : x * 16 + 8, :] = value
        h_ref[x * 16 + 8 : x * 16 + 16, :] = pltpu.roll(value, L - 32, 1)
    b_ref[0] = h_ref[...].T[:32]
    at = pl.multiple_of(((z * NX + x_own) * 2 + c) * 8, 8)
    r = r_ref[pl.ds(at, 8), :][:, :1]
    factor = along * (r * r * r) * (1.0 / width)
    for x in range(NX):
        gains = total(x, feats)
        for f in range(feats):
            k = (x * feats + f) * L
            t_ref[0, :, k : k + L] = total(x, f) - table_ref[:, k : k + L].astype(F32) * factor
            g_ref[0:1, k : k + L] = gains[f : f + 1]


def finish(parts, table, r):
    width = table.shape[1]
    vmem = pl.BlockSpec(memory_space=pltpu.VMEM)
    return pl.pallas_call(
        last_kernel,
        in_specs=[vmem, vmem, vmem],
        out_specs=[vmem] * 3,
        out_shape=[
            jax.ShapeDtypeStruct((1, 8, width), F32),
            jax.ShapeDtypeStruct((1, width), F32),
            jax.ShapeDtypeStruct((1, 32, 64), F32),
        ],
        scratch_shapes=[pltpu.VMEM((64, L), F32)],
        compiler_params=pltpu.CompilerParams(vmem_limit_bytes=8 * MIB),
        cost_estimate=cost(2, 2),
        name="finish",
    )(parts, table, r)


def local(picks, token_ids, segment_ids, row_order, embed_table, norm_gain, position_bias, returned_grad):
    x, z, c = lax.axis_index("x"), lax.axis_index("z"), lax.axis_index("c")
    table, gain, pos, grad = embed_table[0], norm_gain, position_bias[0], returned_grad[0]
    part = table.shape[1] // NX
    sections = lax.axis_size("section")

    def send(value, steps, along):
        pairs = [
            (i * sections + j, (i + steps) % NX * sections + (j + along) % sections)
            for i in range(NX)
            for j in range(sections)
        ]
        return lax.ppermute(value, ("x", "section"), pairs)

    grads = [
        send(lax.dynamic_slice(grad, (0, lax.rem(x + s, NX) * part), (L, part)), s, -1) for s in range(NX)
    ]

    table_then, grads[0], grads[1] = lax.optimization_barrier((table, grads[0], grads[1]))
    ne, r, bvec = prepare(table_then, gain, pos, picks[:32])
    count = 64
    kind = lax.broadcasted_iota(jnp.int32, (count, 3, L), 1)
    note = jnp.where(kind == 0, token_ids, jnp.where(kind == 1, segment_ids, row_order[:, :, None]))
    notes = lax.all_to_all(note, ("z", "x", "c"), 0, 0)

    *acts, normed, probs = forward(notes, ne, bvec)
    pieces = {s: send(acts[s], -s, 1) for s in (2, 1, 3, 0)}
    mine, other = backward(notes, ne, r, gain, picks, normed, probs, grads)
    came = lax.ppermute(other, "c", [(0, 1), (1, 0)])
    handed = jnp.zeros((L, NX * part), BF16)
    for s in (2, 1, 3, 0):
        handed = lax.dynamic_update_slice(handed, pieces[s], (0, lax.rem(x + s, NX) * part))

    parts = lax.all_to_all(join(mine, came), ("z", "x"), 0, 0)
    rows = lax.dynamic_slice(table, (((z * NX + x) * 2 + c) * 8, 0), (8, table.shape[1]))
    return (handed[None],) + tuple(finish(parts, rows, r))


def solution(mesh):
    fine = Mesh(mesh.devices.reshape(8, NX, 2, 4), ("z", "x", "c", "section"))
    dp = ("z", "x", "c")
    placed = (
        P(),
        P("section", dp, None),
        P("section", dp, None),
        P("section", dp),
        P("section", None, None),
        P("section", None),
        P("section", None, None),
        P("section", dp, None),
    )
    mapped = jax.shard_map(
        local,
        mesh=fine,
        in_specs=placed,
        out_specs=(
            P("section", dp, None),
            P("section", dp, None),
            P("section", None),
            P("section", None, None),
        ),
        check_vma=False,
    )
    return lambda *args: mapped(jnp.asarray(bucket_picks()), *args)
```
